256 devices in a mesh: dst: 32 (over y, z), src: 8 (over x, core).
Axes of the slice: x: 4, y: 4, z: 8, core: 2. Of those that a mesh axis runs over, the one named last changes fastest.
Arguments:
- features: bfloat16 [131072, 128], P(('src', 'dst')), may hold values from -64 to 64
- projection: bfloat16 [128, 256], replicated, may hold values from -1 to 1
- source_att: float32 [256], replicated, may hold values from -1.5 to 1.5
- target_att: float32 [256], replicated, may hold values from -1 to 1
- out_bias: float32 [256], replicated, may hold values from -3 to 3
- block_coords: int32 [32, 8, 2, 256], P('dst', 'src'), may hold values from 0 to 127, as said below
- block_words: int32 [32, 8, 256, 16, 128], P('dst', 'src'), may hold values from 0 to 255, as said below
- block_counts: int32 [32, 8], P('dst', 'src'), may hold values from 1 to 256, as said below
Outputs:
- result: bfloat16 [131072, 256], P(('dst', 'src'))
The draws below stay inside these ranges and needn't reach their ends.
Inputs may be any that keep to these rules, and one draw needn't show every extreme that they name: `block_coords`: row entries are below 32 and column entries below 128; the (row, column) pairs of one device's slots are distinct. `block_counts`: at least one device has all 256 slots live. `block_words`: each word holds an 8-bit pattern.
All inputs are finite; a program needn't handle non-finite values.
Results may differ from the reference program's by a relative error of at most 0.019.
Values may be sent and summed in bfloat16 or wider, within the bound.
No kernel may reach another device: no remote copies, remote signals or barrier semaphores. Data moves between devices by JAX's collectives and lax.ppermute only.
A program may use at most 128 MiB of HBM per device.

```python
import math
import jax
import jax.numpy as jnp
from jax import lax

DIN = 128
HEADS = 8
HEAD_DIM = 32
BLOCKS_DEV = 256
NODES = 131072
ROWS_DST = 4096
SRC_ROWS = 16384
N_DST = 32
N_SRC = 8


def model_params(key):
    weight_key = jax.random.fold_in(key, 11)
    attend_key = jax.random.fold_in(key, 12)
    projection = jnp.clip(jax.random.normal(weight_key, (DIN, HEADS * HEAD_DIM), jnp.float32), -5.0, 5.0) / jnp.sqrt(DIN * 1.0)
    source_att = jnp.clip(jax.random.normal(attend_key, (HEADS * HEAD_DIM,), jnp.float32), -5.0, 5.0) / jnp.sqrt(HEAD_DIM * 1.0)
    return (projection, source_att)


def draw_projection(key, part):
    return model_params(key)[0].astype(jnp.bfloat16)


def draw_source_att(key, part):
    return model_params(key)[1]


def draw_features(key, part):
    base_key = jax.random.fold_in(key, 13)
    drawn = jnp.clip(jax.random.normal(base_key, (NODES, DIN), jnp.float32), -6.0, 6.0)
    return drawn.astype(jnp.bfloat16)


def draw_block_coords(key, part):
    col_blocks = SRC_ROWS // 128
    tiles = ROWS_DST // 128 * col_blocks
    keys = jax.random.split(jax.random.fold_in(key, 21), N_DST * N_SRC)

    def pick_slots(one_key):
        return jax.random.permutation(one_key, tiles)[:BLOCKS_DEV]
    picks = jax.vmap(pick_slots)(keys).astype(jnp.int32)
    row_ids = picks // col_blocks
    col_ids = picks % col_blocks
    return jnp.stack([row_ids, col_ids], axis=1).reshape(N_DST, N_SRC, 2, BLOCKS_DEV).astype(jnp.int32)


def draw_block_words(key, part):
    shape = (N_DST, N_SRC, BLOCKS_DEV, 16, 128)
    packed = jnp.full(shape, 255, jnp.int32)
    for layer in range(7):
        piece = jax.random.randint(jax.random.fold_in(key, 31 + layer), shape, 0, 256, jnp.int32)
        packed = packed & piece
    packed = packed.at[0, 0, 0, 0, 0].set(255)
    return packed


def draw_block_counts(key, part):
    device_total = N_DST * N_SRC
    first_pick = jax.random.randint(jax.random.fold_in(key, 41), (device_total,), 1, BLOCKS_DEV + 1, jnp.int32)
    second_pick = jax.random.randint(jax.random.fold_in(key, 42), (device_total,), 1, BLOCKS_DEV + 1, jnp.int32)
    skewed = jnp.maximum(first_pick * second_pick // BLOCKS_DEV, 1)
    busiest = jax.random.randint(jax.random.fold_in(key, 43), (), 0, device_total, jnp.int32)
    skewed = jnp.where(jnp.arange(device_total, dtype=jnp.int32) == busiest, BLOCKS_DEV, skewed)
    return skewed.reshape(N_DST, N_SRC).astype(jnp.int32)


def normal_values(rng, extent, scale, reach, kind=jnp.bfloat16):
    return jnp.clip(scale * jax.random.normal(rng, extent, jnp.float32), -reach, reach).astype(kind)


def setup_inputs(seed: int = 0) -> dict:
    seeds = jax.random.split(jax.random.key(seed), 9)
    return {
        "features": draw_features(jax.random.fold_in(seeds[8], 71), 0),
        "projection": draw_projection(jax.random.fold_in(seeds[8], 71), 0),
        "source_att": draw_source_att(jax.random.fold_in(seeds[8], 71), 0),
        "target_att": normal_values(seeds[3], (HEADS * HEAD_DIM,), HEAD_DIM ** -0.5, 1.0, jnp.float32),
        "out_bias": normal_values(seeds[4], (HEADS * HEAD_DIM,), 0.5, 3.0, jnp.float32),
        "block_coords": draw_block_coords(jax.random.fold_in(seeds[8], 71), 0),
        "block_words": draw_block_words(jax.random.fold_in(seeds[8], 71), 0),
        "block_counts": draw_block_counts(jax.random.fold_in(seeds[8], 71), 0),
    }


def leaky_relu(inputs):
    return jnp.where(inputs > 0, inputs, 0.2 * inputs)


def unpack(packed):
    shifts = jnp.arange(8, dtype=jnp.int32)
    spread = jnp.right_shift(packed[..., :, None, :], shifts[:, None]) & 1
    leading = packed.shape[:-2]
    flattened = spread.reshape(leading + (128, 128))
    return jnp.swapaxes(flattened, -1, -2) > 0


def head_terms(projected, attend):
    return jnp.sum((projected * attend).reshape(projected.shape[0], HEADS, HEAD_DIM), axis=-1)


def reference(features, projection, source_att, target_att, out_bias, block_coords, block_words, block_counts):
    projected = jnp.dot(features, projection, preferred_element_type=jnp.float32)
    source_term = head_terms(projected, source_att)
    target_term = head_terms(projected, target_att)
    values = projected.astype(jnp.bfloat16)
    group_size = math.gcd(BLOCKS_DEV, 16)
    row_blocks = ROWS_DST // 128
    col_blocks = SRC_ROWS // 128
    feature_width = HEADS * HEAD_DIM

    def row_group(group_index):
        row_base = group_index * ROWS_DST
        target_rows = lax.dynamic_slice_in_dim(target_term, row_base, ROWS_DST, 0).reshape(row_blocks, 128, HEADS)
        self_source = lax.dynamic_slice_in_dim(source_term, row_base, ROWS_DST, 0).reshape(row_blocks, 128, HEADS)
        self_values = lax.dynamic_slice_in_dim(values, row_base, ROWS_DST, 0).reshape(row_blocks, 128, HEADS, HEAD_DIM)
        self_score = leaky_relu(target_rows + self_source)

        def column_inputs(column):
            col_base = column * SRC_ROWS
            source_cols = lax.dynamic_slice_in_dim(source_term, col_base, SRC_ROWS, 0).reshape(col_blocks, 128, HEADS)
            value_cols = lax.dynamic_slice_in_dim(values, col_base, SRC_ROWS, 0).reshape(col_blocks, 128, HEADS, HEAD_DIM)
            return source_cols, value_cols, block_coords[group_index, column], block_words[group_index, column], block_counts[group_index, column]

        def group_scores(step_index, coords, packed_words, live_count, source_cols):
            first_slot = step_index * group_size
            row_ids = lax.dynamic_slice_in_dim(coords[0], first_slot, group_size)
            col_ids = lax.dynamic_slice_in_dim(coords[1], first_slot, group_size)
            packed = lax.dynamic_slice_in_dim(packed_words, first_slot, group_size, 0)
            valid_slot = (first_slot + jnp.arange(group_size, dtype=jnp.int32)) < live_count
            edge_mask = unpack(packed) & valid_slot[:, None, None]
            scores = leaky_relu(target_rows[row_ids][:, :, None, :] + source_cols[col_ids][:, None, :, :])
            return row_ids, col_ids, edge_mask, scores

        def tile_max(column):
            source_cols, value_cols, coords, packed_words, live_count = column_inputs(column)

            def max_step(step_index, maxima):
                row_ids, col_ids, edge_mask, scores = group_scores(step_index, coords, packed_words, live_count, source_cols)
                block_max = jnp.max(jnp.where(edge_mask[..., None], scores, -jnp.inf), axis=2)
                return maxima.at[row_ids].max(block_max)

            start_max = jnp.full((row_blocks, 128, HEADS), -jnp.inf, jnp.float32)
            return lax.fori_loop(0, (live_count + group_size - 1) // group_size, max_step, start_max)

        maxima = jnp.max(lax.map(tile_max, jnp.arange(N_SRC, dtype=jnp.int32)), axis=0)
        maxima = jnp.maximum(maxima, self_score)

        def tile_sum(column):
            source_cols, value_cols, coords, packed_words, live_count = column_inputs(column)

            def sum_step(step_index, carry_state):
                weighted, denominator = carry_state
                row_ids, col_ids, edge_mask, scores = group_scores(step_index, coords, packed_words, live_count, source_cols)
                weight = jnp.where(edge_mask[..., None], jnp.exp(scores - maxima[row_ids][:, :, None, :]), 0.0)
                denominator = denominator.at[row_ids].add(jnp.sum(weight, axis=2))
                rounded = lax.optimization_barrier(weight.astype(jnp.bfloat16))
                contrib = jnp.einsum('gabh,gbhc->gahc', rounded.astype(jnp.float32), value_cols[col_ids].astype(jnp.float32))
                weighted = weighted.at[row_ids].add(contrib)
                return weighted, denominator

            start_state = (jnp.zeros((row_blocks, 128, HEADS, HEAD_DIM), jnp.float32), jnp.zeros((row_blocks, 128, HEADS), jnp.float32))
            return lax.fori_loop(0, (live_count + group_size - 1) // group_size, sum_step, start_state)

        all_weighted, all_denominator = lax.map(tile_sum, jnp.arange(N_SRC, dtype=jnp.int32))
        weighted = jnp.sum(all_weighted, axis=0)
        denominator = jnp.sum(all_denominator, axis=0)
        self_weight = jnp.exp(self_score - maxima)
        denominator = denominator + self_weight
        self_rounded = lax.optimization_barrier(self_weight.astype(jnp.bfloat16))
        weighted = weighted + self_rounded.astype(jnp.float32)[..., None] * self_values.astype(jnp.float32)
        mixed_rows = (weighted / denominator[..., None]).reshape(ROWS_DST, feature_width) + out_bias
        return jax.nn.elu(mixed_rows).astype(jnp.bfloat16)

    outputs = lax.map(row_group, jnp.arange(N_DST, dtype=jnp.int32))
    return outputs.reshape(NODES, feature_width)
```

```python
import jax
import jax.numpy as jnp
import numpy as np
from jax import lax
from jax.experimental import pallas as pl
from jax.experimental.pallas import tpu as pltpu
from jax.sharding import PartitionSpec as P

HEADS = 8
HEAD_DIM = 32
BLOCK = 128
WIDTH = HEADS * HEAD_DIM
AUX = 48
RANGE = 60.0
LOWEST = -3.0e38
BF = jnp.bfloat16
F32 = jnp.float32
NT = (((1,), (1,)), ((), ()))
TN = (((0,), (0,)), ((), ()))


def leaky(v):
    return jnp.maximum(v, 0.2 * v)


def den_lane(head):
    return (64 if (head // 2) % 2 == 0 else 0) + head % 2


def constants():
    spread = np.zeros((16, BLOCK), np.float32)
    for b in range(BLOCK):
        spread[b // 8, b] = 0.5 ** (b % 8)
    keep = np.zeros((HEADS, 16, BLOCK), np.float32)
    ones = np.zeros((HEADS, 16, BLOCK), np.float32)
    for h in range(HEADS):
        keep[h, :, (h % 4) * 32 : (h % 4) * 32 + 32] = 1.0
        ones[h, :, den_lane(h)] = 1.0
    fan = np.zeros((16, 2 * HEADS * BLOCK), np.float32)
    for k in range(16):
        fan[k, k * BLOCK : (k + 1) * BLOCK] = 1.0
    pick = np.zeros((4, HEADS, BLOCK), np.float32)
    for h in range(HEADS):
        pick[h // 2, h, den_lane(h)] = 1.0
    head_fan = np.zeros((2 * HEADS, WIDTH), np.float32)
    for h in range(HEADS):
        head_fan[h, h * 32 : h * 32 + 32] = 1.0
        head_fan[HEADS + h, h * 32 : h * 32 + 32] = 1.0
    return [jnp.asarray(x, BF) for x in (spread, keep, ones, fan, pick, head_fan)]


def halves(x):
    high = x.astype(BF).astype(F32)
    return high, (x - high).astype(BF).astype(F32)


def block_kernel(
    coords, count, fg, proj, wst, terms, words, spread, keep, ones, fan, pick,
    out, values, src, src_a, src_b, fac_a, fac_b, acc, hi, lo, col_t, col_s, col_m,
):
    nodes = fg.shape[0]
    rows = terms.shape[1]
    row_blocks = rows // BLOCK
    shards = out.shape[0]
    own = rows // shards
    live = count[0]

    def project(i, _):
        at = pl.ds(pl.multiple_of(i * 512, 512), 512)
        f = fg[at, :]
        values[at, :] = jnp.dot(f, proj[...], preferred_element_type=F32).astype(BF)
        both = lax.dot_general(wst[...], f, NT, preferred_element_type=F32)
        src[:, at] = both[:HEADS] + both[HEADS:]
        return 0

    lax.fori_loop(0, nodes // 512, project, 0)
    top = jnp.max(src[...], axis=1, keepdims=True)
    self_low = jnp.min(terms[HEADS:, :], axis=1, keepdims=True)
    narrow = jnp.max(top - self_low) <= RANGE

    def clear(i, _):
        acc[i] = jnp.zeros(acc.shape[1:], F32)
        return 0

    lax.fori_loop(0, row_blocks, clear, 0)

    def edges(slot):
        w = words[slot].astype(F32).astype(BF)
        x = lax.dot_general(w, spread[...], TN, preferred_element_type=F32)
        return (x.astype(jnp.int32) & 1).astype(F32)

    def add_pair(r, g, ws, v):
        parts = []
        for h in (2 * g, 2 * g + 1):
            vt = v[:, (h // 4) * BLOCK : (h // 4 + 1) * BLOCK].reshape(8, 16, BLOCK)
            parts.append((vt * keep[h][None] + ones[h][None]).reshape(BLOCK, BLOCK))
        acc[r, g] += jnp.dot(
            jnp.concatenate(ws, axis=1), jnp.concatenate(parts, axis=0), preferred_element_type=F32
        )

    @pl.when(narrow)
    def _():
        src_a[...] = jnp.exp(src[...] - top)
        src_b[...] = jnp.exp(0.2 * (src[...] - top))
        upper = terms[:HEADS, :] + top
        high, low = halves(leaky(upper))
        hi[...] = high
        lo[...] = low
        shift = high + low
        col_a = jnp.exp(upper - shift)
        col_b = jnp.exp(0.2 * upper - shift)
        both = jnp.concatenate([col_a, col_b], axis=0).astype(BF)
        for r in range(row_blocks):
            wide = lax.dot_general(
                both[:, r * BLOCK : (r + 1) * BLOCK], fan[...], TN, preferred_element_type=F32
            ).astype(BF)
            for h in range(HEADS):
                fac_a[r, h] = wide[:, h * BLOCK : (h + 1) * BLOCK].reshape(8, 16, BLOCK)
                fac_b[r, h] = wide[:, (HEADS + h) * BLOCK : (HEADS + h + 1) * BLOCK].reshape(8, 16, BLOCK)

        def step(slot, _):
            r = coords[0, slot]
            q = pl.multiple_of(coords[1, slot] * BLOCK, BLOCK)
            mask = edges(slot).astype(BF).reshape(8, 16, BLOCK)
            sa = src_a[:, pl.ds(q, BLOCK)]
            sb = src_b[:, pl.ds(q, BLOCK)]
            v = values[pl.ds(q, BLOCK), :]
            for g in range(4):
                ws = []
                for h in (2 * g, 2 * g + 1):
                    a = jnp.broadcast_to(sa[h : h + 1, :], (16, BLOCK)).astype(BF)[None]
                    b = jnp.broadcast_to(sb[h : h + 1, :], (16, BLOCK)).astype(BF)[None]
                    w = jnp.maximum(fac_a[r, h] * a, fac_b[r, h] * b) * mask
                    ws.append(w.reshape(BLOCK, BLOCK))
                add_pair(r, g, ws, v)
            return 0

        lax.fori_loop(0, live, step, 0)

    @pl.when(jnp.logical_not(narrow))
    def _():
        col_s[...] = jnp.full(col_s.shape, LOWEST, F32)

        def masked_max(slot, _):
            r = pl.multiple_of(coords[0, slot] * BLOCK, BLOCK)
            q = pl.multiple_of(coords[1, slot] * BLOCK, BLOCK)
            edge = edges(slot) > 0
            s = src[:, pl.ds(q, BLOCK)]
            best = [
                jnp.max(jnp.where(edge, s[h : h + 1, :], LOWEST), axis=1, keepdims=True)
                for h in range(HEADS)
            ]
            at = pl.ds(r, BLOCK)
            col_s[at, :] = jnp.maximum(col_s[at, :], jnp.concatenate(best, axis=1))
            return 0

        lax.fori_loop(0, live, masked_max, 0)
        for r in range(row_blocks):
            at = slice(r * BLOCK, (r + 1) * BLOCK)
            t = terms[:HEADS, at]
            exact = jnp.maximum(leaky(t + terms[HEADS:, at]), leaky(t + col_s[at, :].T))
            high, low = halves(exact)
            hi[:, at] = high
            lo[:, at] = low
            col_m[at, :] = (high + low).T
            col_t[at, :] = t.T

        def step(slot, _):
            r = coords[0, slot]
            at = pl.ds(pl.multiple_of(r * BLOCK, BLOCK), BLOCK)
            q = pl.multiple_of(coords[1, slot] * BLOCK, BLOCK)
            edge = edges(slot) > 0
            s = src[:, pl.ds(q, BLOCK)]
            v = values[pl.ds(q, BLOCK), :]
            t = col_t[at, :]
            m = col_m[at, :]
            for g in range(4):
                ws = []
                for h in (2 * g, 2 * g + 1):
                    score = leaky(t[:, h : h + 1] + s[h : h + 1, :]) - m[:, h : h + 1]
                    ws.append(jnp.where(edge, jnp.exp(score), 0.0).astype(BF))
                add_pair(r, g, ws, v)
            return 0

        lax.fori_loop(0, live, step, 0)

    lane = lax.broadcasted_iota(jnp.int32, (BLOCK, BLOCK), 1)
    per = own // BLOCK

    def wide_rows(x):
        return jnp.concatenate([x[:, : own // 2], x[:, own // 2 :]], axis=0).astype(BF)

    def finish(j, _):
        dens = []
        for k in range(per):
            r = j * per + k
            a = [acc[r, g] for g in range(4)]
            at = slice(k * BLOCK, (k + 1) * BLOCK)
            out[j, at, :BLOCK] = jnp.where(lane < 64, a[0], a[1]).astype(BF)
            out[j, at, BLOCK:] = jnp.where(lane < 64, a[2], a[3]).astype(BF)
            dens.append(
                sum(
                    lax.dot_general(pick[g], a[g].astype(BF), NT, preferred_element_type=F32)
                    for g in range(4)
                )
            )
        at = pl.ds(pl.multiple_of(j * own, own), own)
        out[j, own : own + 16, :] = wide_rows(jnp.concatenate(dens, axis=1))
        out[j, own + 16 : own + 32, :] = wide_rows(hi[:, at])
        out[j, own + 32 : own + 48, :] = wide_rows(lo[:, at])
        return 0

    lax.fori_loop(0, shards, finish, 0)


def combine_kernel(parts, feats, proj, terms, bias, head_fan, out):
    shards = parts.shape[0]
    own = feats.shape[0]

    def tall(x):
        x = x.astype(F32)
        return jnp.concatenate([x[:HEADS], x[HEADS:]], axis=1)

    dens, shifts = [], []
    for j in range(shards):
        dens.append(tall(parts[j, own : own + 16, :]))
        shifts.append(tall(parts[j, own + 16 : own + 32, :]) + tall(parts[j, own + 32 : own + 48, :]))
    score = leaky(terms[:HEADS, :] + terms[HEADS:, :])
    m = score
    for s in shifts:
        m = jnp.maximum(m, s)
    own_weight = jnp.exp(score - m)
    total = own_weight
    scales = []
    for d, s in zip(dens, shifts):
        scale = jnp.exp(s - m)
        scales.append(scale)
        total = total + scale * d
    inverse = 1.0 / total

    def fanned(x):
        high, low = halves(x)
        both = jnp.concatenate([high, low], axis=0).astype(BF)
        return lax.dot_general(both, head_fan[...], TN, preferred_element_type=F32)

    values = jnp.dot(feats[...], proj[...], preferred_element_type=F32).astype(BF).astype(F32)
    mixed = fanned(own_weight * inverse) * values + bias[...]
    for j in range(shards):
        mixed = mixed + fanned(scales[j] * inverse) * parts[j, :own, :].astype(F32)
    out[...] = jnp.where(mixed > 0, mixed, jnp.exp(jnp.minimum(mixed, 0.0)) - 1.0).astype(BF)


def on_device(
    features, projection, source_att, target_att, out_bias, block_coords, block_words, block_counts
):
    dst_count = lax.axis_size("dst")
    src_count = lax.axis_size("src")
    own_rows = features.shape[0]
    rows = own_rows * src_count
    nodes = own_rows * dst_count
    spread, keep, ones, fan, pick, head_fan = constants()
    gathered = lax.all_gather(features, "dst", axis=0, tiled=True)

    moves = []
    for d in range(dst_count):
        for s in range(src_count):
            block = s * dst_count + d
            moves.append((d * src_count + s, block))
    own_feats = lax.ppermute(features, ("dst", "src"), moves)
    atts = jnp.stack([target_att, source_att])
    folded = (projection.astype(F32)[None] * atts[:, None, :]).reshape(2, -1, HEADS, HEAD_DIM)
    folded = jnp.sum(folded, axis=-1).transpose(0, 2, 1).reshape(2 * HEADS, -1)
    own_terms = lax.dot_general(
        folded, own_feats.astype(F32), NT, precision=lax.Precision.HIGHEST,
        preferred_element_type=F32,
    )
    row_terms = lax.all_gather(own_terms, "src", axis=1, tiled=True)
    ws = folded[HEADS:]
    ws_high = lax.reduce_precision(ws, 8, 7)
    wst = jnp.concatenate([ws_high, ws - ws_high], axis=0).astype(BF)

    smem = pl.BlockSpec(memory_space=pltpu.SMEM)
    vmem = pl.BlockSpec(memory_space=pltpu.VMEM)
    row_blocks = rows // BLOCK
    parts = pl.pallas_call(
        block_kernel,
        name="edge_blocks",
        out_shape=jax.ShapeDtypeStruct((src_count, own_rows + AUX, WIDTH), BF),
        in_specs=[smem, smem] + [vmem] * 10,
        out_specs=vmem,
        scratch_shapes=[
            pltpu.VMEM((nodes, WIDTH), BF),
            pltpu.VMEM((HEADS, nodes), F32),
            pltpu.VMEM((HEADS, nodes), F32),
            pltpu.VMEM((HEADS, nodes), F32),
            pltpu.VMEM((row_blocks, HEADS, 8, 16, BLOCK), BF),
            pltpu.VMEM((row_blocks, HEADS, 8, 16, BLOCK), BF),
            pltpu.VMEM((row_blocks, 4, BLOCK, BLOCK), F32),
            pltpu.VMEM((HEADS, rows), F32),
            pltpu.VMEM((HEADS, rows), F32),
            pltpu.VMEM((rows, HEADS), F32),
            pltpu.VMEM((rows, HEADS), F32),
            pltpu.VMEM((rows, HEADS), F32),
        ],
        compiler_params=pltpu.CompilerParams(vmem_limit_bytes=60 * 2**20),
    )(
        block_coords[0, 0], block_counts[0], gathered, projection, wst, row_terms,
        block_words[0, 0], spread, keep, ones, fan, pick,
    )
    received = lax.all_to_all(parts, "src", 0, 0)
    return pl.pallas_call(
        combine_kernel,
        name="combine_rows",
        out_shape=jax.ShapeDtypeStruct((own_rows, WIDTH), BF),
        in_specs=[vmem] * 6,
        out_specs=vmem,
        compiler_params=pltpu.CompilerParams(vmem_limit_bytes=60 * 2**20),
    )(received, own_feats, projection, own_terms, out_bias[None], head_fan)


def solution(mesh):
    placed = (
        P(("src", "dst"), None),
        P(),
        P(),
        P(),
        P(),
        P("dst", "src", None, None),
        P("dst", "src", None, None, None),
        P("dst", "src"),
    )
    return jax.shard_map(
        on_device, mesh=mesh, in_specs=placed, out_specs=P(("dst", "src"), None), check_vma=False
    )
```

```python
import jax
import jax.numpy as jnp
import numpy as np
from jax import lax
from jax.experimental import pallas as pl
from jax.experimental.pallas import tpu as pltpu
from jax.sharding import PartitionSpec as P

HEADS = 8
HEAD_DIM = 32
BLOCK = 128
WIDTH = HEADS * HEAD_DIM
AUX = 48
STRIDE = 8
PARTS = 4
Y_STEPS = (0, 1, 3, 2)
Z_STEPS = (0, 1, 7, 2, 6, 3, 5, 4)
LOWEST = -3.0e38
BF = jnp.bfloat16
F32 = jnp.float32
NT = (((1,), (1,)), ((), ()))
TN = (((0,), (0,)), ((), ()))


def leaky(v):
    return jnp.maximum(v, 0.2 * v)


def constants():
    spread = np.zeros((16, BLOCK), np.float32)
    for b in range(BLOCK):
        spread[b // 8, b] = 0.5 ** (b % 8)
    keep = np.zeros((2, 16, BLOCK), np.float32)
    ones = np.zeros((2, 2, BLOCK, BLOCK), np.float32)
    for p in range(2):
        for lane in range(BLOCK):
            keep[p, :, lane] = float((lane % 64) // 32 == p)
        for t in range(2):
            ones[t, p, :, 4 * t + p] = 1.0
            ones[t, p, :, 4 * t + 2 + p] = 1.0
    pick = np.zeros((HEADS, BLOCK), np.float32)
    fan = np.zeros((HEADS, HEADS * BLOCK), np.float32)
    head_fan = np.zeros((2 * HEADS, WIDTH), np.float32)
    for h in range(HEADS):
        pick[h, h] = 1.0
        fan[h, h * BLOCK : (h + 1) * BLOCK] = 1.0
        head_fan[h, h * 32 : h * 32 + 32] = 1.0
        head_fan[HEADS + h, h * 32 : h * 32 + 32] = 1.0
    return [jnp.asarray(x, BF) for x in (spread, keep, ones, fan, pick, head_fan)]


def halves(x):
    high = x.astype(BF).astype(F32)
    return high, (x - high).astype(BF).astype(F32)


def terms_kernel(feats, proj, atts, head_fan, terms, wst):
    weights = proj[...].astype(F32)
    fold = head_fan[:HEADS, :].astype(F32)
    folded = [
        lax.dot_general(
            fold, weights * atts[k : k + 1, :], NT,
            precision=lax.Precision.HIGHEST, preferred_element_type=F32,
        )
        for k in range(2)
    ]
    terms[...] = lax.dot_general(
        jnp.concatenate(folded, axis=0), feats[...].astype(F32), NT,
        precision=lax.Precision.HIGHEST, preferred_element_type=F32,
    )
    high, low = halves(folded[1])
    wst[...] = jnp.concatenate([high, low], axis=0).astype(BF)


def mask_kernel(part, count, words, spread, masks):
    slots = masks.shape[0]
    live = jnp.clip(count[0] - part * slots, 0, slots)

    def edges(i, _):
        for k in range(STRIDE):
            slot = i * STRIDE + k
            w = words[slot] * jnp.where(slot < live, 1, 0)
            x = lax.dot_general(
                w.astype(F32).astype(BF), spread[...], TN, preferred_element_type=F32
            )
            bits = (x.astype(jnp.int32) & 1).astype(F32).astype(BF)
            masks[slot] = bits.reshape(8, 16, BLOCK)
        return 0

    lax.fori_loop(0, pl.cdiv(live, STRIDE), edges, 0)


def source_marks(terms):
    return jnp.max(jnp.max(terms[:, HEADS:, :], axis=0), axis=1, keepdims=True)


def factor_kernel(terms, fan, factors):
    mark = source_marks(terms)
    shards, _, own = terms.shape
    per = own // BLOCK
    for j in range(shards):
        factor = jnp.exp(jnp.minimum(-0.8 * (terms[j, :HEADS, :] + mark), 80.0)).astype(BF)
        for k in range(per):
            wide = lax.dot_general(
                factor[:, k * BLOCK : (k + 1) * BLOCK], fan[...], TN, preferred_element_type=F32
            ).astype(BF)
            for h in range(HEADS):
                factors[j * per + k, h] = wide[:, h * BLOCK : (h + 1) * BLOCK].reshape(8, 16, BLOCK)


def block_kernel(coords, count, place, *refs):
    pieces = refs[:8]
    proj, wst, terms = refs[8:11]
    masks_in = refs[11 : 11 + PARTS]
    (
        factors_in, keep, ones, pick,
        out, values, src, src_a, src_b, masks, factors, acc0, acc1, acc_d,
        hi, lo, col_t, col_s, col_m, sems,
    ) = refs[11 + PARTS :]
    accs = (acc0, acc1)
    piece_rows = pieces[0].shape[0] // 4
    shards, _, own = terms.shape
    per = own // BLOCK
    row_blocks = shards * per
    live = count[0]
    part = masks.shape[0] // PARTS
    copies = [
        pltpu.make_async_copy(masks_in[k], masks.at[k * part : (k + 1) * part], sems.at[k])
        for k in range(PARTS)
    ]
    copies.append(pltpu.make_async_copy(factors_in, factors, sems.at[PARTS]))
    for copy in copies:
        copy.start()

    zero = jnp.zeros((BLOCK, BLOCK), F32)
    for k, dz in enumerate(Z_STEPS):
        for m, dy in enumerate(Y_STEPS):
            y = (place[0] + 4 - dy) % 4
            z = (place[1] + 8 - dz) % 8
            at = pl.ds(pl.multiple_of((y * 8 + z) * piece_rows, piece_rows), piece_rows)
            f = pieces[k][m * piece_rows : (m + 1) * piece_rows, :]
            values[at, :] = jnp.dot(f, proj[...], preferred_element_type=F32).astype(BF)
            both = lax.dot_general(wst[...], f, NT, preferred_element_type=F32)
            src[:, at] = both[:HEADS] + both[HEADS:]
    for r in range(row_blocks):
        for acc in (acc0, acc1, acc_d):
            acc[r] = zero

    top = jnp.max(src[...], axis=1, keepdims=True)
    mark = source_marks(terms)
    self_low = jnp.min(jnp.min(terms[:, HEADS:, :], axis=0), axis=1, keepdims=True)
    row_low = jnp.min(jnp.min(terms[:, :HEADS, :], axis=0), axis=1, keepdims=True) + mark
    narrow = (
        (jnp.max(top - mark) <= 40.0)
        & (jnp.max(mark - self_low) <= 60.0)
        & (jnp.min(row_low) >= -50.0)
    )
    for copy in copies:
        copy.wait()

    lane = lax.broadcasted_iota(jnp.int32, (BLOCK, BLOCK), 1)
    left = lane < 64
    second = (lane & 2) > 0

    def slot_of(slot):
        used = slot < live
        r = jnp.where(used, coords[0, slot], 0)
        q = jnp.where(used, coords[1, slot], 0)
        return r, q

    def nodes_of(q):
        return pl.ds(pl.multiple_of(q * BLOCK, BLOCK), BLOCK)

    def add_block(r, q, weight_of):
        dens = []
        for t in range(2):
            ws = [weight_of(h) for h in range(4 * t, 4 * t + 4)]
            lhs = jnp.concatenate(
                [jnp.concatenate(ws[:2], axis=1), jnp.concatenate(ws[2:], axis=1)], axis=0
            )
            vt = values[nodes_of(q), t * BLOCK : (t + 1) * BLOCK].reshape(8, 16, BLOCK)
            kept = jnp.concatenate(
                [
                    jnp.where(keep[p][None] > 0, vt, jnp.zeros_like(vt)).reshape(BLOCK, BLOCK)
                    for p in range(2)
                ],
                axis=0,
            )
            rhs = jnp.concatenate([kept, ones[t].reshape(2 * BLOCK, BLOCK)], axis=1)
            x = jnp.dot(lhs, rhs, preferred_element_type=F32)
            dens.append(jnp.where(second, x[BLOCK:, BLOCK:], x[:BLOCK, BLOCK:]))
            accs[t][r] += jnp.where(left, x[:BLOCK, :BLOCK], x[BLOCK:, :BLOCK])
        acc_d[r] += dens[0] + dens[1]

    @pl.when(narrow)
    def _():
        for b in range(src_a.shape[0]):
            gap = src[:, b * BLOCK : (b + 1) * BLOCK] - mark
            src_a[b] = jnp.exp(gap)
            src_b[b] = jnp.exp(0.2 * gap)
        for j in range(shards):
            high, low = halves(terms[j, :HEADS, :] + mark)
            hi[j] = high
            lo[j] = low

        def step(i, _):
            for k in range(STRIDE):
                slot = i * STRIDE + k
                r, q = slot_of(slot)

                def weight_of(h):
                    a = src_a[q, pl.ds(h, 16, stride=0), :].astype(BF)[None]
                    b = src_b[q, pl.ds(h, 16, stride=0), :].astype(BF)[None]
                    w = jnp.maximum(factors[r, h] * b, a) * masks[slot]
                    return w.reshape(BLOCK, BLOCK)

                add_block(r, q, weight_of)
            return 0

        lax.fori_loop(0, pl.cdiv(live, STRIDE), step, 0)

    @pl.when(jnp.logical_not(narrow))
    def _():
        col_s[...] = jnp.full(col_s.shape, LOWEST, F32)

        def edge_of(slot):
            return masks[slot].reshape(BLOCK, BLOCK).astype(F32) > 0

        def masked_max(slot, _):
            r, q = slot_of(slot)
            edge = edge_of(slot)
            s = src[:, nodes_of(q)]
            best = [
                jnp.max(jnp.where(edge, s[h : h + 1, :], LOWEST), axis=1, keepdims=True)
                for h in range(HEADS)
            ]
            at = nodes_of(r)
            col_s[at, :] = jnp.maximum(col_s[at, :], jnp.concatenate(best, axis=1))
            return 0

        lax.fori_loop(0, live, masked_max, 0)
        for r in range(row_blocks):
            at = slice(r * BLOCK, (r + 1) * BLOCK)
            j = r // per
            inner = slice((r % per) * BLOCK, (r % per + 1) * BLOCK)
            t = terms[j, :HEADS, inner]
            exact = jnp.maximum(leaky(t + terms[j, HEADS:, inner]), leaky(t + col_s[at, :].T))
            high, low = halves(exact)
            hi[j, :, inner] = high
            lo[j, :, inner] = low
            col_m[at, :] = (high + low).T
            col_t[at, :] = t.T

        def step(slot, _):
            r, q = slot_of(slot)
            edge = edge_of(slot)
            s = src[:, nodes_of(q)]
            t = col_t[nodes_of(r), :]
            m = col_m[nodes_of(r), :]

            def weight_of(h):
                score = leaky(t[:, h : h + 1] + s[h : h + 1, :]) - m[:, h : h + 1]
                return jnp.where(edge, jnp.exp(score), 0.0).astype(BF)

            add_block(r, q, weight_of)
            return 0

        lax.fori_loop(0, live, step, 0)

    def wide_rows(x):
        return jnp.concatenate([x[:, : own // 2], x[:, own // 2 :]], axis=0).astype(BF)

    def finish(j, _):
        dens = []
        for k in range(per):
            r = j * per + k
            at = slice(k * BLOCK, (k + 1) * BLOCK)
            out[j, at, :BLOCK] = acc0[r].astype(BF)
            out[j, at, BLOCK:] = acc1[r].astype(BF)
            dens.append(
                lax.dot_general(pick[...], acc_d[r].astype(BF), NT, preferred_element_type=F32)
            )
        out[j, own : own + 16, :] = wide_rows(jnp.concatenate(dens, axis=1))
        out[j, own + 16 : own + 32, :] = wide_rows(hi[j])
        out[j, own + 32 : own + 48, :] = wide_rows(lo[j])
        return 0

    lax.fori_loop(0, shards, finish, 0)


def combine_kernel(parts, feats, proj, terms, bias, head_fan, out):
    shards = parts.shape[0]
    own = feats.shape[0]

    def tall(x):
        x = x.astype(F32)
        return jnp.concatenate([x[:HEADS], x[HEADS:]], axis=1)

    dens, shifts = [], []
    for j in range(shards):
        dens.append(tall(parts[j, own : own + 16, :]))
        shifts.append(tall(parts[j, own + 16 : own + 32, :]) + tall(parts[j, own + 32 : own + 48, :]))
    score = leaky(terms[:HEADS, :] + terms[HEADS:, :])
    m = score
    for s in shifts:
        m = jnp.maximum(m, s)
    own_weight = jnp.exp(score - m)
    total = own_weight
    scales = []
    for d, s in zip(dens, shifts):
        scale = jnp.exp(s - m)
        scales.append(scale)
        total = total + scale * d
    inverse = 1.0 / total

    def fanned(x):
        high, low = halves(x)
        both = jnp.concatenate([high, low], axis=0).astype(BF)
        return lax.dot_general(both, head_fan[...], TN, preferred_element_type=F32)

    values = jnp.dot(feats[...], proj[...], preferred_element_type=F32).astype(BF).astype(F32)
    mixed = fanned(own_weight * inverse) * values + bias[...]
    for j in range(shards):
        mixed = mixed + fanned(scales[j] * inverse) * parts[j, :own, :].astype(F32)
    out[...] = jnp.where(mixed > 0, mixed, jnp.exp(jnp.minimum(mixed, 0.0)) - 1.0).astype(BF)


def on_device(
    features, projection, source_att, target_att, out_bias, block_coords, block_words, block_counts
):
    dst_count = lax.axis_size("dst")
    src_count = lax.axis_size("src")
    own_rows = features.shape[0]
    rows = own_rows * src_count
    nodes = own_rows * dst_count
    slots = block_coords.shape[3]
    row_blocks = rows // BLOCK
    spread, keep, ones, fan, pick, head_fan = constants()
    smem = pl.BlockSpec(memory_space=pltpu.SMEM)
    vmem = pl.BlockSpec(memory_space=pltpu.VMEM)
    anywhere = pl.BlockSpec(memory_space=pl.ANY)
    params = pltpu.CompilerParams(vmem_limit_bytes=60 * 2**20)
    words = block_words[0, 0]

    def shift(x, dy, dz):
        return lax.ppermute(
            x,
            "dst",
            [(y * 8 + z, (y + dy) % 4 * 8 + (z + dz) % 8) for y in range(4) for z in range(8)],
        )

    def masks_of(part, count):
        def body(*refs):
            mask_kernel(part, *refs)

        return pl.pallas_call(
            body,
            name="edge_masks",
            grid=(1,),
            out_shape=jax.ShapeDtypeStruct((slots // PARTS, 8, 16, BLOCK), BF),
            in_specs=[
                smem,
                pl.BlockSpec((slots // PARTS, 16, BLOCK), lambda i: (part, 0, 0)),
                vmem,
            ],
            out_specs=vmem,
            compiler_params=params,
        )(count, words, spread)

    moves = []
    for d in range(dst_count):
        for s in range(src_count):
            moves.append((d * src_count + s, s * dst_count + d))
    own_feats = lax.ppermute(features, ("dst", "src"), moves)
    near = [features if dy == 0 else shift(features, dy, 0) for dy in Y_STEPS]
    count = block_counts[0]
    masks = [masks_of(0, count)]
    near, masks[0], count = lax.optimization_barrier((near, masks[0], count))
    column = jnp.concatenate(near, axis=0)
    arrived = {0: column, 1: shift(column, 0, 1), 7: shift(column, 0, 7)}
    own_terms, wst = pl.pallas_call(
        terms_kernel,
        name="own_terms",
        out_shape=[
            jax.ShapeDtypeStruct((2 * HEADS, own_rows), F32),
            jax.ShapeDtypeStruct((2 * HEADS, features.shape[1]), BF),
        ],
        in_specs=[vmem] * 4,
        out_specs=[vmem, vmem],
        compiler_params=params,
    )(own_feats, projection, jnp.stack([target_att, source_att]), head_fan)
    row_terms = lax.all_to_all(
        jnp.broadcast_to(own_terms[None], (src_count,) + own_terms.shape), "src", 0, 0
    )
    arrived[1], arrived[7], row_terms, count = lax.optimization_barrier(
        (arrived[1], arrived[7], row_terms, count)
    )
    arrived[2], arrived[6] = shift(arrived[1], 0, 1), shift(arrived[7], 0, 7)
    masks.append(masks_of(1, count))
    arrived[2], arrived[6], masks[1], count = lax.optimization_barrier(
        (arrived[2], arrived[6], masks[1], count)
    )
    arrived[3], arrived[5] = shift(arrived[2], 0, 1), shift(arrived[6], 0, 7)
    masks.append(masks_of(2, count))
    arrived[3], arrived[5], masks[2], count, row_terms = lax.optimization_barrier(
        (arrived[3], arrived[5], masks[2], count, row_terms)
    )
    arrived[4] = shift(arrived[3], 0, 1)
    masks.append(masks_of(3, count))
    factor_shape = (row_blocks, HEADS, 8, 16, BLOCK)
    factors = pl.pallas_call(
        factor_kernel,
        name="row_factors",
        out_shape=jax.ShapeDtypeStruct(factor_shape, BF),
        in_specs=[vmem] * 2,
        out_specs=vmem,
        compiler_params=params,
    )(row_terms, fan)
    place = lax.axis_index("dst")
    place = jnp.stack([place // 8, place % 8]).astype(jnp.int32)
    parts = pl.pallas_call(
        block_kernel,
        name="edge_blocks",
        out_shape=jax.ShapeDtypeStruct((src_count, own_rows + AUX, WIDTH), BF),
        in_specs=[smem] * 3 + [vmem] * 11 + [anywhere] * (PARTS + 1) + [vmem] * 3,
        out_specs=vmem,
        scratch_shapes=[
            pltpu.VMEM((nodes, WIDTH), BF),
            pltpu.VMEM((HEADS, nodes), F32),
            pltpu.VMEM((nodes // BLOCK, HEADS, BLOCK), F32),
            pltpu.VMEM((nodes // BLOCK, HEADS, BLOCK), F32),
            pltpu.VMEM((slots, 8, 16, BLOCK), BF),
            pltpu.VMEM(factor_shape, BF),
        ]
        + [pltpu.VMEM((row_blocks, BLOCK, BLOCK), F32)] * 3
        + [pltpu.VMEM((src_count, HEADS, own_rows), F32)] * 2
        + [pltpu.VMEM((rows, HEADS), F32)] * 3
        + [pltpu.SemaphoreType.DMA((PARTS + 1,))],
        compiler_params=params,
    )(
        block_coords[0, 0], count, place, *[arrived[dz] for dz in Z_STEPS],
        projection, wst, row_terms, *masks, factors, keep, ones, pick,
    )
    received = lax.all_to_all(parts, "src", 0, 0)
    return pl.pallas_call(
        combine_kernel,
        name="combine_rows",
        out_shape=jax.ShapeDtypeStruct((own_rows, WIDTH), BF),
        in_specs=[vmem] * 6,
        out_specs=vmem,
        compiler_params=params,
    )(received, own_feats, projection, own_terms, out_bias[None], head_fan)


def solution(mesh):
    placed = (
        P(("src", "dst"), None),
        P(),
        P(),
        P(),
        P(),
        P("dst", "src", None, None),
        P("dst", "src", None, None, None),
        P("dst", "src"),
    )
    return jax.shard_map(
        on_device, mesh=mesh, in_specs=placed, out_specs=P(("dst", "src"), None), check_vma=False
    )
```

```python
import jax
import jax.numpy as jnp
import numpy as np
from jax import lax
from jax.experimental import pallas as pl
from jax.experimental.pallas import tpu as pltpu
from jax.sharding import PartitionSpec as P

HEADS = 8
HEAD_DIM = 32
BLOCK = 128
WIDTH = HEADS * HEAD_DIM
AUX = 48
STRIDE = 8
PARTS = 4
Y_STEPS = (0, 1, 3, 2)
PIECES = tuple((dz, Y_STEPS) for dz in (0, 1, 7, 2, 6, 3, 5)) + ((4, Y_STEPS[:2]), (4, Y_STEPS[2:]))
X_STEPS = (2, 1, 3, 0)
LOWEST = -3.0e38
BF = jnp.bfloat16
F32 = jnp.float32
NT = (((1,), (1,)), ((), ()))
TN = (((0,), (0,)), ((), ()))


def leaky(v):
    return jnp.maximum(v, 0.2 * v)


def constants():
    spread = np.zeros((16, BLOCK), np.float32)
    for b in range(BLOCK):
        spread[b // 8, b] = 0.5 ** (b % 8)
    keep = np.zeros((2, 16, BLOCK), np.float32)
    ones = np.zeros((2, 2, BLOCK, BLOCK), np.float32)
    for p in range(2):
        for lane in range(BLOCK):
            keep[p, :, lane] = float((lane % 64) // 32 == p)
        for t in range(2):
            ones[t, p, :, 4 * t + p] = 1.0
            ones[t, p, :, 4 * t + 2 + p] = 1.0
    pick = np.zeros((HEADS, BLOCK), np.float32)
    fan = np.zeros((HEADS, HEADS * BLOCK), np.float32)
    head_fan = np.zeros((2 * HEADS, WIDTH), np.float32)
    for h in range(HEADS):
        pick[h, h] = 1.0
        fan[h, h * BLOCK : (h + 1) * BLOCK] = 1.0
        head_fan[h, h * 32 : h * 32 + 32] = 1.0
        head_fan[HEADS + h, h * 32 : h * 32 + 32] = 1.0
    return [jnp.asarray(x, BF) for x in (spread, keep, ones, fan, pick, head_fan)]


def halves(x):
    high = x.astype(BF).astype(F32)
    return high, (x - high).astype(BF).astype(F32)


def terms_kernel(feats, proj, atts, head_fan, terms, wst):
    weights = proj[...].astype(F32)
    fold = head_fan[:HEADS, :].astype(F32)
    folded = [
        lax.dot_general(
            fold, weights * atts[k : k + 1, :], NT,
            precision=lax.Precision.HIGHEST, preferred_element_type=F32,
        )
        for k in range(2)
    ]
    terms[...] = lax.dot_general(
        jnp.concatenate(folded, axis=0), feats[...].astype(F32), NT,
        precision=lax.Precision.HIGHEST, preferred_element_type=F32,
    )
    high, low = halves(folded[1])
    wst[...] = jnp.concatenate([high, low], axis=0).astype(BF)


def mask_kernel(part, count, words, spread, masks):
    slots = masks.shape[0]
    live = jnp.clip(count[0] - part * slots, 0, slots)

    def edges(i, _):
        for k in range(STRIDE):
            slot = i * STRIDE + k
            w = words[slot] * jnp.where(slot < live, 1, 0)
            x = lax.dot_general(
                w.astype(F32).astype(BF), spread[...], TN, preferred_element_type=F32
            )
            bits = (x.astype(jnp.int32) & 1).astype(F32).astype(BF)
            masks[slot] = bits.reshape(8, 16, BLOCK)
        return 0

    lax.fori_loop(0, pl.cdiv(live, STRIDE), edges, 0)


def source_marks(terms):
    return jnp.max(jnp.max(terms[:, HEADS:, :], axis=0), axis=1, keepdims=True)


def factor_kernel(terms, fan, factors):
    mark = source_marks(terms)
    shards, _, own = terms.shape
    per = own // BLOCK
    for j in range(shards):
        factor = jnp.exp(jnp.minimum(-0.8 * (terms[j, :HEADS, :] + mark), 80.0)).astype(BF)
        for k in range(per):
            wide = lax.dot_general(
                factor[:, k * BLOCK : (k + 1) * BLOCK], fan[...], TN, preferred_element_type=F32
            ).astype(BF)
            for h in range(HEADS):
                factors[j * per + k, h] = wide[:, h * BLOCK : (h + 1) * BLOCK].reshape(8, 16, BLOCK)


def block_kernel(coords, count, place, *refs):
    pieces = refs[: len(PIECES)]
    refs = refs[len(PIECES) :]
    proj, wst, terms = refs[:3]
    masks_in = refs[3 : 3 + PARTS]
    (
        factors_in, keep, ones, pick,
        *outs, values, src, src_a, src_b, masks, factors, acc0, acc1, acc_d,
        hi, lo, col_t, col_s, col_m, sems,
    ) = refs[3 + PARTS :]
    accs = (acc0, acc1)
    piece_rows = pieces[0].shape[0] // len(Y_STEPS)
    shards, _, own = terms.shape
    per = own // BLOCK
    row_blocks = shards * per
    live = count[0]
    part = masks.shape[0] // PARTS
    copies = [
        pltpu.make_async_copy(masks_in[k], masks.at[k * part : (k + 1) * part], sems.at[k])
        for k in range(PARTS)
    ]
    copies.append(pltpu.make_async_copy(factors_in, factors, sems.at[PARTS]))
    for copy in copies:
        copy.start()

    zero = jnp.zeros((BLOCK, BLOCK), F32)
    for k, (dz, y_steps) in enumerate(PIECES):
        for m, dy in enumerate(y_steps):
            y = (place[0] + 4 - dy) % 4
            z = (place[1] + 8 - dz) % 8
            at = pl.ds(pl.multiple_of((y * 8 + z) * piece_rows, piece_rows), piece_rows)
            f = pieces[k][m * piece_rows : (m + 1) * piece_rows, :]
            values[at, :] = jnp.dot(f, proj[...], preferred_element_type=F32).astype(BF)
            both = lax.dot_general(wst[...], f, NT, preferred_element_type=F32)
            src[:, at] = both[:HEADS] + both[HEADS:]
    for r in range(row_blocks):
        for acc in (acc0, acc1, acc_d):
            acc[r] = zero

    top = jnp.max(src[...], axis=1, keepdims=True)
    mark = source_marks(terms)
    self_low = jnp.min(jnp.min(terms[:, HEADS:, :], axis=0), axis=1, keepdims=True)
    row_low = jnp.min(jnp.min(terms[:, :HEADS, :], axis=0), axis=1, keepdims=True) + mark
    narrow = (
        (jnp.max(top - mark) <= 40.0)
        & (jnp.max(mark - self_low) <= 60.0)
        & (jnp.min(row_low) >= -50.0)
    )
    for copy in copies:
        copy.wait()

    lane = lax.broadcasted_iota(jnp.int32, (BLOCK, BLOCK), 1)
    left = lane < 64
    second = (lane & 2) > 0

    def slot_of(slot):
        used = slot < live
        r = jnp.where(used, coords[0, slot], 0)
        q = jnp.where(used, coords[1, slot], 0)
        return r, q

    def nodes_of(q):
        return pl.ds(pl.multiple_of(q * BLOCK, BLOCK), BLOCK)

    def add_block(r, q, weight_of):
        dens = []
        for t in range(2):
            ws = [weight_of(h) for h in range(4 * t, 4 * t + 4)]
            lhs = jnp.concatenate(
                [jnp.concatenate(ws[:2], axis=1), jnp.concatenate(ws[2:], axis=1)], axis=0
            )
            vt = values[nodes_of(q), t * BLOCK : (t + 1) * BLOCK].reshape(8, 16, BLOCK)
            kept = jnp.concatenate(
                [
                    jnp.where(keep[p][None] > 0, vt, jnp.zeros_like(vt)).reshape(BLOCK, BLOCK)
                    for p in range(2)
                ],
                axis=0,
            )
            rhs = jnp.concatenate([kept, ones[t].reshape(2 * BLOCK, BLOCK)], axis=1)
            x = jnp.dot(lhs, rhs, preferred_element_type=F32)
            dens.append(jnp.where(second, x[BLOCK:, BLOCK:], x[:BLOCK, BLOCK:]))
            accs[t][r] += jnp.where(left, x[:BLOCK, :BLOCK], x[BLOCK:, :BLOCK])
        acc_d[r] += dens[0] + dens[1]

    @pl.when(narrow)
    def _():
        for b in range(src_a.shape[0]):
            gap = src[:, b * BLOCK : (b + 1) * BLOCK] - mark
            src_a[b] = jnp.exp(gap)
            src_b[b] = jnp.exp(0.2 * gap)
        for j in range(shards):
            high, low = halves(terms[j, :HEADS, :] + mark)
            hi[j] = high
            lo[j] = low

        def step(i, _):
            for k in range(STRIDE):
                slot = i * STRIDE + k
                r, q = slot_of(slot)

                def weight_of(h):
                    a = src_a[q, pl.ds(h, 16, stride=0), :].astype(BF)[None]
                    b = src_b[q, pl.ds(h, 16, stride=0), :].astype(BF)[None]
                    w = jnp.maximum(factors[r, h] * b, a) * masks[slot]
                    return w.reshape(BLOCK, BLOCK)

                add_block(r, q, weight_of)
            return 0

        lax.fori_loop(0, pl.cdiv(live, STRIDE), step, 0)

    @pl.when(jnp.logical_not(narrow))
    def _():
        col_s[...] = jnp.full(col_s.shape, LOWEST, F32)

        def edge_of(slot):
            return masks[slot].reshape(BLOCK, BLOCK).astype(F32) > 0

        def masked_max(slot, _):
            r, q = slot_of(slot)
            edge = edge_of(slot)
            s = src[:, nodes_of(q)]
            best = [
                jnp.max(jnp.where(edge, s[h : h + 1, :], LOWEST), axis=1, keepdims=True)
                for h in range(HEADS)
            ]
            at = nodes_of(r)
            col_s[at, :] = jnp.maximum(col_s[at, :], jnp.concatenate(best, axis=1))
            return 0

        lax.fori_loop(0, live, masked_max, 0)
        for r in range(row_blocks):
            at = slice(r * BLOCK, (r + 1) * BLOCK)
            j = r // per
            inner = slice((r % per) * BLOCK, (r % per + 1) * BLOCK)
            t = terms[j, :HEADS, inner]
            exact = jnp.maximum(leaky(t + terms[j, HEADS:, inner]), leaky(t + col_s[at, :].T))
            high, low = halves(exact)
            hi[j, :, inner] = high
            lo[j, :, inner] = low
            col_m[at, :] = (high + low).T
            col_t[at, :] = t.T

        def step(slot, _):
            r, q = slot_of(slot)
            edge = edge_of(slot)
            s = src[:, nodes_of(q)]
            t = col_t[nodes_of(r), :]
            m = col_m[nodes_of(r), :]

            def weight_of(h):
                score = leaky(t[:, h : h + 1] + s[h : h + 1, :]) - m[:, h : h + 1]
                return jnp.where(edge, jnp.exp(score), 0.0).astype(BF)

            add_block(r, q, weight_of)
            return 0

        lax.fori_loop(0, live, step, 0)

    for i, out in enumerate(outs):
        j = (place[2] + X_STEPS[i % 4]) % 4 * 2 + (1 - place[3] if i < 4 else place[3])
        dens = []
        for k in range(per):
            r = j * per + k
            at = slice(k * BLOCK, (k + 1) * BLOCK)
            out[at, :BLOCK] = acc0[r].astype(BF)
            out[at, BLOCK:] = acc1[r].astype(BF)
            dens.append(
                lax.dot_general(pick[...], acc_d[r].astype(BF), NT, preferred_element_type=F32)
            )
        out[own : own + 16, :] = flat(jnp.concatenate(dens, axis=1))
        out[own + 16 : own + 32, :] = flat(hi[j])
        out[own + 32 : own + 48, :] = flat(lo[j])


def tall(x):
    x = x.astype(F32)
    return jnp.concatenate([x[:HEADS], x[HEADS:]], axis=1)


def flat(x):
    half = x.shape[1] // 2
    return jnp.concatenate([x[:, :half], x[:, half:]], axis=0).astype(BF)


def fanned(x, head_fan):
    high, low = halves(x)
    both = jnp.concatenate([high, low], axis=0).astype(BF)
    return lax.dot_general(both, head_fan[...], TN, preferred_element_type=F32)


def pair_kernel(kept, got, head_fan, out):
    own = out.shape[0] - AUX
    read = (kept, got)
    den = [tall(x[own : own + 16, :]) for x in read]
    high = [tall(x[own + 16 : own + 32, :]) for x in read]
    low = [tall(x[own + 32 : own + 48, :]) for x in read]
    shift = [h + l for h, l in zip(high, low)]
    m = jnp.maximum(shift[0], shift[1])
    scale = [jnp.exp(x - m) for x in shift]
    total = sum(fanned(k, head_fan) * x[:own, :].astype(F32) for k, x in zip(scale, read))
    out[:own, :] = total.astype(BF)
    first = shift[0] >= shift[1]
    out[own : own + 16, :] = flat(scale[0] * den[0] + scale[1] * den[1])
    out[own + 16 : own + 32, :] = flat(jnp.where(first, high[0], high[1]))
    out[own + 32 : own + 48, :] = flat(jnp.where(first, low[0], low[1]))


def combine_kernel(*refs):
    parts = refs[:4]
    feats, proj, terms, bias, head_fan, out = refs[4:]
    own = feats.shape[0]
    dens, shifts = [], []
    for part in parts:
        dens.append(tall(part[own : own + 16, :]))
        shifts.append(tall(part[own + 16 : own + 32, :]) + tall(part[own + 32 : own + 48, :]))
    score = leaky(terms[:HEADS, :] + terms[HEADS:, :])
    m = score
    for s in shifts:
        m = jnp.maximum(m, s)
    own_weight = jnp.exp(score - m)
    total = own_weight
    scales = []
    for d, s in zip(dens, shifts):
        scale = jnp.exp(s - m)
        scales.append(scale)
        total = total + scale * d
    inverse = 1.0 / total
    values = jnp.dot(feats[...], proj[...], preferred_element_type=F32).astype(BF).astype(F32)
    mixed = fanned(own_weight * inverse, head_fan) * values + bias[...]
    for part, scale in zip(parts, scales):
        mixed = mixed + fanned(scale * inverse, head_fan) * part[:own, :].astype(F32)
    out[...] = jnp.where(mixed > 0, mixed, jnp.exp(jnp.minimum(mixed, 0.0)) - 1.0).astype(BF)


def on_device(
    features, projection, source_att, target_att, out_bias, block_coords, block_words, block_counts
):
    dst_count = lax.axis_size("dst")
    src_count = lax.axis_size("src")
    own_rows = features.shape[0]
    rows = own_rows * src_count
    nodes = own_rows * dst_count
    slots = block_coords.shape[3]
    row_blocks = rows // BLOCK
    spread, keep, ones, fan, pick, head_fan = constants()
    smem = pl.BlockSpec(memory_space=pltpu.SMEM)
    vmem = pl.BlockSpec(memory_space=pltpu.VMEM)
    anywhere = pl.BlockSpec(memory_space=pl.ANY)
    params = pltpu.CompilerParams(vmem_limit_bytes=60 * 2**20)
    words = block_words[0, 0]

    def shift(x, dy, dz):
        return lax.ppermute(
            x,
            "dst",
            [(y * 8 + z, (y + dy) % 4 * 8 + (z + dz) % 8) for y in range(4) for z in range(8)],
        )

    def masks_of(part, count):
        def body(*refs):
            mask_kernel(part, *refs)

        return pl.pallas_call(
            body,
            name="edge_masks",
            grid=(1,),
            out_shape=jax.ShapeDtypeStruct((slots // PARTS, 8, 16, BLOCK), BF),
            in_specs=[
                smem,
                pl.BlockSpec((slots // PARTS, 16, BLOCK), lambda i: (part, 0, 0)),
                vmem,
            ],
            out_specs=vmem,
            compiler_params=params,
        )(count, words, spread)

    moves = []
    for d in range(dst_count):
        for s in range(src_count):
            moves.append((d * src_count + s, s * dst_count + d))
    own_feats = lax.ppermute(features, ("dst", "src"), moves)
    near = [features if dy == 0 else shift(features, dy, 0) for dy in Y_STEPS]
    count = block_counts[0]
    masks = [masks_of(0, count)]
    near, masks[0], count, own_feats = lax.optimization_barrier(
        (near, masks[0], count, own_feats)
    )
    column = jnp.concatenate(near, axis=0)
    arrived = {0: column, 1: shift(column, 0, 1), 7: shift(column, 0, 7)}
    own_terms, wst = pl.pallas_call(
        terms_kernel,
        name="own_terms",
        out_shape=[
            jax.ShapeDtypeStruct((2 * HEADS, own_rows), F32),
            jax.ShapeDtypeStruct((2 * HEADS, features.shape[1]), BF),
        ],
        in_specs=[vmem] * 4,
        out_specs=[vmem, vmem],
        compiler_params=params,
    )(own_feats, projection, jnp.stack([target_att, source_att]), head_fan)
    masks.append(masks_of(1, count))
    arrived[1], arrived[7], own_terms, masks, count = lax.optimization_barrier(
        (arrived[1], arrived[7], own_terms, masks, count)
    )
    arrived[2], arrived[6] = shift(arrived[1], 0, 1), shift(arrived[7], 0, 7)
    row_terms = lax.all_to_all(
        jnp.broadcast_to(own_terms[None], (src_count,) + own_terms.shape), "src", 0, 0
    )
    arrived[2], arrived[6], row_terms, count = lax.optimization_barrier(
        (arrived[2], arrived[6], row_terms, count)
    )
    arrived[3], arrived[5] = shift(arrived[2], 0, 1), shift(arrived[6], 0, 7)
    factor_shape = (row_blocks, HEADS, 8, 16, BLOCK)
    factors = pl.pallas_call(
        factor_kernel,
        name="row_factors",
        out_shape=jax.ShapeDtypeStruct(factor_shape, BF),
        in_specs=[vmem] * 2,
        out_specs=vmem,
        compiler_params=params,
    )(row_terms, fan)
    masks.append(masks_of(2, count))
    arrived[3], arrived[5], factors, masks, count = lax.optimization_barrier(
        (arrived[3], arrived[5], factors, masks, count)
    )
    middle = column.shape[0] // 2
    last = [shift(arrived[3][:middle], 0, 1), shift(arrived[5][middle:], 0, 7)]
    masks.append(masks_of(3, count))
    at_dst, at_src = lax.axis_index("dst"), lax.axis_index("src")
    place = jnp.stack([at_dst // 8, at_dst % 8, at_src // 2, at_src % 2]).astype(jnp.int32)
    part_shape = jax.ShapeDtypeStruct((own_rows + AUX, WIDTH), BF)
    parts = pl.pallas_call(
        block_kernel,
        name="edge_blocks",
        out_shape=[part_shape] * src_count,
        in_specs=[smem] * 3 + [vmem] * (len(PIECES) + 3) + [anywhere] * (PARTS + 1) + [vmem] * 3,
        out_specs=[vmem] * src_count,
        scratch_shapes=[
            pltpu.VMEM((nodes, WIDTH), BF),
            pltpu.VMEM((HEADS, nodes), F32),
            pltpu.VMEM((nodes // BLOCK, HEADS, BLOCK), F32),
            pltpu.VMEM((nodes // BLOCK, HEADS, BLOCK), F32),
            pltpu.VMEM((slots, 8, 16, BLOCK), BF),
            pltpu.VMEM(factor_shape, BF),
        ]
        + [pltpu.VMEM((row_blocks, BLOCK, BLOCK), F32)] * 3
        + [pltpu.VMEM((src_count, HEADS, own_rows), F32)] * 2
        + [pltpu.VMEM((rows, HEADS), F32)] * 3
        + [pltpu.SemaphoreType.DMA((PARTS + 1,))],
        compiler_params=params,
    )(
        block_coords[0, 0], count, place, *[arrived[dz] for dz, _ in PIECES[:7]], *last,
        projection, wst, row_terms, *masks, factors, keep, ones, pick,
    )
    swap = [(i, i ^ 1) for i in range(src_count)]
    got = [lax.ppermute(x, "src", swap) for x in parts[:4]]
    sums = []
    for k, kept, other in zip(X_STEPS, parts[4:], got):
        x = pl.pallas_call(
            pair_kernel,
            name="pair_sums",
            out_shape=part_shape,
            in_specs=[vmem] * 3,
            out_specs=vmem,
            compiler_params=params,
        )(kept, other, head_fan)
        if k:
            x = lax.ppermute(
                x, "src", [(i, (i + 2 * k) % src_count) for i in range(src_count)]
            )
        sums.append(x)
    return pl.pallas_call(
        combine_kernel,
        name="combine_rows",
        out_shape=jax.ShapeDtypeStruct((own_rows, WIDTH), BF),
        in_specs=[vmem] * 9,
        out_specs=vmem,
        compiler_params=params,
    )(*sums, own_feats, projection, own_terms, out_bias[None], head_fan)


def solution(mesh):
    placed = (
        P(("src", "dst"), None),
        P(),
        P(),
        P(),
        P(),
        P("dst", "src", None, None),
        P("dst", "src", None, None, None),
        P("dst", "src"),
    )
    return jax.shard_map(
        on_device, mesh=mesh, in_specs=placed, out_specs=P(("dst", "src"), None), check_vma=False
    )
```

```python
import jax
import jax.numpy as jnp
import numpy as np
from jax import lax
from jax.experimental import pallas as pl
from jax.experimental.pallas import tpu as pltpu
from jax.sharding import PartitionSpec as P

HEADS = 8
HEAD_DIM = 32
BLOCK = 128
WIDTH = HEADS * HEAD_DIM
AUX = 48
STRIDE = 16
PARTS = 4
Y_STEPS = (0, 1, 3, 2)
PIECES = tuple((dz, Y_STEPS) for dz in (0, 1, 7, 2, 6, 3, 5)) + ((4, Y_STEPS[:2]), (4, Y_STEPS[2:]))
X_STEPS = (2, 1, 3, 0)
LOWEST = -3.0e38
BF = jnp.bfloat16
F32 = jnp.float32
NT = (((1,), (1,)), ((), ()))
TN = (((0,), (0,)), ((), ()))


def leaky(v):
    return jnp.maximum(v, 0.2 * v)


def constants():
    spread = np.zeros((8, 16, 8, BLOCK), np.float32)
    for k in range(8):
        for b in range(BLOCK):
            spread[k, b // 8, k, b] = 0.5 ** (b % 8)
    spread = spread.reshape(BLOCK, 8 * BLOCK)
    keep = np.zeros((2, 16, BLOCK), np.float32)
    ones = np.zeros((2, 2, BLOCK, BLOCK), np.float32)
    for p in range(2):
        for lane in range(BLOCK):
            keep[p, :, lane] = float((lane % 64) // 32 == p)
        for t in range(2):
            ones[t, p, :, 4 * t + p] = 1.0
            ones[t, p, :, 4 * t + 2 + p] = 1.0
    pick = np.zeros((HEADS, BLOCK), np.float32)
    fan = np.zeros((HEADS, HEADS * BLOCK), np.float32)
    head_fan = np.zeros((2 * HEADS, WIDTH), np.float32)
    for h in range(HEADS):
        pick[h, h] = 1.0
        fan[h, h * BLOCK : (h + 1) * BLOCK] = 1.0
        head_fan[h, h * 32 : h * 32 + 32] = 1.0
        head_fan[HEADS + h, h * 32 : h * 32 + 32] = 1.0
    return [jnp.asarray(x, BF) for x in (spread, keep, ones, fan, pick, head_fan)]


def halves(x):
    high = x.astype(BF).astype(F32)
    return high, (x - high).astype(BF).astype(F32)


def terms_kernel(feats, proj, atts, head_fan, terms, wst):
    weights = proj[...].astype(F32)
    fold = head_fan[:HEADS, :].astype(F32)
    folded = [
        lax.dot_general(
            fold, weights * atts[k : k + 1, :], NT,
            precision=lax.Precision.HIGHEST, preferred_element_type=F32,
        )
        for k in range(2)
    ]
    terms[...] = lax.dot_general(
        jnp.concatenate(folded, axis=0), feats[...].astype(F32), NT,
        precision=lax.Precision.HIGHEST, preferred_element_type=F32,
    )
    high, low = halves(folded[1])
    wst[...] = jnp.concatenate([high, low], axis=0).astype(BF)


def mask_kernel(part, count, words, spread, masks):
    slots = masks.shape[0]
    live = jnp.clip(count[0] - part * slots, 0, slots)

    def edges(i, _):
        for g in range(4):
            at = pl.multiple_of(i * 32 + g * 8, 8)
            index = at + lax.broadcasted_iota(jnp.int32, (8, 16, BLOCK), 0)
            w = jnp.where(index < live, words[pl.ds(at, 8)], 0)
            w = w.astype(F32).reshape(BLOCK, BLOCK).T.astype(BF)
            x = jnp.dot(w, spread[...], preferred_element_type=F32)
            bits = (x.astype(jnp.int32) & 1).astype(F32).astype(BF)
            for k in range(8):
                masks[at + k] = bits[:, k * BLOCK : (k + 1) * BLOCK].reshape(8, 16, BLOCK)
        return 0

    lax.fori_loop(0, pl.cdiv(live, 32), edges, 0)


def source_marks(terms):
    return jnp.max(jnp.max(terms[:, HEADS:, :], axis=0), axis=1, keepdims=True)


def factor_kernel(terms, fan, factors):
    mark = source_marks(terms)
    shards, _, own = terms.shape
    per = own // BLOCK
    for j in range(shards):
        factor = jnp.exp(jnp.minimum(-0.8 * (terms[j, :HEADS, :] + mark), 80.0)).astype(BF)
        for k in range(per):
            wide = lax.dot_general(
                factor[:, k * BLOCK : (k + 1) * BLOCK], fan[...], TN, preferred_element_type=F32
            ).astype(BF)
            for h in range(HEADS):
                factors[j * per + k, h] = wide[:, h * BLOCK : (h + 1) * BLOCK].reshape(8, 16, BLOCK)


def block_kernel(coords, count, place, *refs):
    pieces = refs[: len(PIECES)]
    refs = refs[len(PIECES) :]
    proj, wst, terms = refs[:3]
    masks_in = refs[3 : 3 + PARTS]
    (
        factors_in, keep, ones, pick,
        *outs, values, src, src_a, src_b, masks, factors, acc0, acc1, acc_d,
        hi, lo, col_t, col_s, col_m, sems,
    ) = refs[3 + PARTS :]
    accs = (acc0, acc1)
    piece_rows = pieces[0].shape[0] // len(Y_STEPS)
    shards, _, own = terms.shape
    per = own // BLOCK
    row_blocks = shards * per
    live = count[0]
    part = masks.shape[0] // PARTS
    copies = [
        pltpu.make_async_copy(masks_in[k], masks.at[k * part : (k + 1) * part], sems.at[k])
        for k in range(PARTS)
    ]
    copies.append(pltpu.make_async_copy(factors_in, factors, sems.at[PARTS]))
    for copy in copies:
        copy.start()

    zero = jnp.zeros((BLOCK, BLOCK), F32)
    for k, (dz, y_steps) in enumerate(PIECES):
        for m, dy in enumerate(y_steps):
            y = (place[0] + 4 - dy) % 4
            z = (place[1] + 8 - dz) % 8
            at = pl.ds(pl.multiple_of((y * 8 + z) * piece_rows, piece_rows), piece_rows)
            f = pieces[k][m * piece_rows : (m + 1) * piece_rows, :]
            values[at, :] = jnp.dot(f, proj[...], preferred_element_type=F32).astype(BF)
            both = lax.dot_general(wst[...], f, NT, preferred_element_type=F32)
            src[:, at] = both[:HEADS] + both[HEADS:]
    for r in range(row_blocks):
        for acc in (acc0, acc1, acc_d):
            acc[r] = zero

    top = jnp.max(src[...], axis=1, keepdims=True)
    mark = source_marks(terms)
    self_low = jnp.min(jnp.min(terms[:, HEADS:, :], axis=0), axis=1, keepdims=True)
    row_low = jnp.min(jnp.min(terms[:, :HEADS, :], axis=0), axis=1, keepdims=True) + mark
    narrow = (
        (jnp.max(top - mark) <= 40.0)
        & (jnp.max(mark - self_low) <= 60.0)
        & (jnp.min(row_low) >= -50.0)
    )
    for copy in copies:
        copy.wait()

    lane = lax.broadcasted_iota(jnp.int32, (BLOCK, BLOCK), 1)
    left = lane < 64
    second = (lane & 2) > 0

    def slot_of(slot):
        used = slot < live
        r = jnp.where(used, coords[0, slot], 0)
        q = jnp.where(used, coords[1, slot], 0)
        return r, q

    def nodes_of(q):
        return pl.ds(pl.multiple_of(q * BLOCK, BLOCK), BLOCK)

    def add_block(r, q, weight_of):
        dens = []
        for t in range(2):
            ws = [weight_of(h) for h in range(4 * t, 4 * t + 4)]
            lhs = jnp.concatenate(
                [jnp.concatenate(ws[:2], axis=1), jnp.concatenate(ws[2:], axis=1)], axis=0
            )
            vt = values[nodes_of(q), t * BLOCK : (t + 1) * BLOCK].reshape(8, 16, BLOCK)
            kept = jnp.concatenate(
                [
                    jnp.where(keep[p][None] > 0, vt, jnp.zeros_like(vt)).reshape(BLOCK, BLOCK)
                    for p in range(2)
                ],
                axis=0,
            )
            rhs = jnp.concatenate([kept, ones[t].reshape(2 * BLOCK, BLOCK)], axis=1)
            x = jnp.dot(lhs, rhs, preferred_element_type=F32)
            dens.append(jnp.where(second, x[BLOCK:, BLOCK:], x[:BLOCK, BLOCK:]))
            accs[t][r] += jnp.where(left, x[:BLOCK, :BLOCK], x[BLOCK:, :BLOCK])
        acc_d[r] += dens[0] + dens[1]

    @pl.when(narrow)
    def _():
        for b in range(src_a.shape[0]):
            gap = src[:, b * BLOCK : (b + 1) * BLOCK] - mark
            src_a[b] = jnp.exp(gap)
            src_b[b] = jnp.exp(0.2 * gap)
        for j in range(shards):
            high, low = halves(terms[j, :HEADS, :] + mark)
            hi[j] = high
            lo[j] = low

        def step(i, _):
            for k in range(STRIDE):
                slot = i * STRIDE + k
                r, q = slot_of(slot)

                def weight_of(h):
                    a = src_a[q, pl.ds(h, 16, stride=0), :].astype(BF)[None]
                    b = src_b[q, pl.ds(h, 16, stride=0), :].astype(BF)[None]
                    w = jnp.maximum(factors[r, h] * b, a) * masks[slot]
                    return w.reshape(BLOCK, BLOCK)

                add_block(r, q, weight_of)
            return 0

        lax.fori_loop(0, pl.cdiv(live, STRIDE), step, 0)

    @pl.when(jnp.logical_not(narrow))
    def _():
        col_s[...] = jnp.full(col_s.shape, LOWEST, F32)

        def edge_of(slot):
            return masks[slot].reshape(BLOCK, BLOCK).astype(F32) > 0

        def masked_max(slot, _):
            r, q = slot_of(slot)
            edge = edge_of(slot)
            s = src[:, nodes_of(q)]
            best = [
                jnp.max(jnp.where(edge, s[h : h + 1, :], LOWEST), axis=1, keepdims=True)
                for h in range(HEADS)
            ]
            at = nodes_of(r)
            col_s[at, :] = jnp.maximum(col_s[at, :], jnp.concatenate(best, axis=1))
            return 0

        lax.fori_loop(0, live, masked_max, 0)
        for r in range(row_blocks):
            at = slice(r * BLOCK, (r + 1) * BLOCK)
            j = r // per
            inner = slice((r % per) * BLOCK, (r % per + 1) * BLOCK)
            t = terms[j, :HEADS, inner]
            exact = jnp.maximum(leaky(t + terms[j, HEADS:, inner]), leaky(t + col_s[at, :].T))
            high, low = halves(exact)
            hi[j, :, inner] = high
            lo[j, :, inner] = low
            col_m[at, :] = (high + low).T
            col_t[at, :] = t.T

        def step(slot, _):
            r, q = slot_of(slot)
            edge = edge_of(slot)
            s = src[:, nodes_of(q)]
            t = col_t[nodes_of(r), :]
            m = col_m[nodes_of(r), :]

            def weight_of(h):
                score = leaky(t[:, h : h + 1] + s[h : h + 1, :]) - m[:, h : h + 1]
                return jnp.where(edge, jnp.exp(score), 0.0).astype(BF)

            add_block(r, q, weight_of)
            return 0

        lax.fori_loop(0, live, step, 0)

    for i, out in enumerate(outs):
        j = (place[2] + X_STEPS[i % 4]) % 4 * 2 + (1 - place[3] if i < 4 else place[3])
        dens = []
        for k in range(per):
            r = j * per + k
            at = slice(k * BLOCK, (k + 1) * BLOCK)
            out[at, :BLOCK] = acc0[r].astype(BF)
            out[at, BLOCK:] = acc1[r].astype(BF)
            dens.append(
                lax.dot_general(pick[...], acc_d[r].astype(BF), NT, preferred_element_type=F32)
            )
        out[own : own + 16, :] = flat(jnp.concatenate(dens, axis=1))
        out[own + 16 : own + 32, :] = flat(hi[j])
        out[own + 32 : own + 48, :] = flat(lo[j])


def tall(x):
    x = x.astype(F32)
    return jnp.concatenate([x[:HEADS], x[HEADS:]], axis=1)


def flat(x):
    half = x.shape[1] // 2
    return jnp.concatenate([x[:, :half], x[:, half:]], axis=0).astype(BF)


def fanned(x, head_fan):
    high, low = halves(x)
    both = jnp.concatenate([high, low], axis=0).astype(BF)
    return lax.dot_general(both, head_fan[...], TN, preferred_element_type=F32)


def pair_kernel(kept, got, head_fan, out):
    own = out.shape[0] - AUX
    read = (kept, got)
    den = [tall(x[own : own + 16, :]) for x in read]
    high = [tall(x[own + 16 : own + 32, :]) for x in read]
    low = [tall(x[own + 32 : own + 48, :]) for x in read]
    shift = [h + l for h, l in zip(high, low)]
    m = jnp.maximum(shift[0], shift[1])
    scale = [jnp.exp(x - m) for x in shift]
    equal = jnp.max(jnp.abs(shift[0] - shift[1])) == 0.0

    @pl.when(equal)
    def _():
        out[:own, :] = (kept[:own, :].astype(F32) + got[:own, :].astype(F32)).astype(BF)

    @pl.when(jnp.logical_not(equal))
    def _():
        total = sum(fanned(k, head_fan) * x[:own, :].astype(F32) for k, x in zip(scale, read))
        out[:own, :] = total.astype(BF)

    first = shift[0] >= shift[1]
    out[own : own + 16, :] = flat(scale[0] * den[0] + scale[1] * den[1])
    out[own + 16 : own + 32, :] = flat(jnp.where(first, high[0], high[1]))
    out[own + 32 : own + 48, :] = flat(jnp.where(first, low[0], low[1]))


def combine_kernel(*refs):
    parts = refs[:4]
    feats, proj, terms, bias, head_fan, out = refs[4:]
    own = feats.shape[0]
    dens, shifts = [], []
    for part in parts:
        dens.append(tall(part[own : own + 16, :]))
        shifts.append(tall(part[own + 16 : own + 32, :]) + tall(part[own + 32 : own + 48, :]))
    score = leaky(terms[:HEADS, :] + terms[HEADS:, :])
    m = score
    for s in shifts:
        m = jnp.maximum(m, s)
    own_weight = jnp.exp(score - m)
    total = own_weight
    scales = []
    for d, s in zip(dens, shifts):
        scale = jnp.exp(s - m)
        scales.append(scale)
        total = total + scale * d
    inverse = 1.0 / total
    values = jnp.dot(feats[...], proj[...], preferred_element_type=F32).astype(BF).astype(F32)
    mixed = fanned(own_weight * inverse, head_fan) * values + bias[...]
    for part, scale in zip(parts, scales):
        mixed = mixed + fanned(scale * inverse, head_fan) * part[:own, :].astype(F32)
    out[...] = jnp.where(mixed > 0, mixed, jnp.exp(jnp.minimum(mixed, 0.0)) - 1.0).astype(BF)


def on_device(
    features, projection, source_att, target_att, out_bias, block_coords, block_words, block_counts
):
    dst_count = lax.axis_size("dst")
    src_count = lax.axis_size("src")
    own_rows = features.shape[0]
    rows = own_rows * src_count
    nodes = own_rows * dst_count
    slots = block_coords.shape[3]
    row_blocks = rows // BLOCK
    spread, keep, ones, fan, pick, head_fan = constants()
    smem = pl.BlockSpec(memory_space=pltpu.SMEM)
    vmem = pl.BlockSpec(memory_space=pltpu.VMEM)
    anywhere = pl.BlockSpec(memory_space=pl.ANY)
    params = pltpu.CompilerParams(vmem_limit_bytes=60 * 2**20)
    words = block_words[0, 0]

    def shift(x, dy, dz):
        return lax.ppermute(
            x,
            "dst",
            [(y * 8 + z, (y + dy) % 4 * 8 + (z + dz) % 8) for y in range(4) for z in range(8)],
        )

    def masks_of(part, count):
        def body(*refs):
            mask_kernel(part, *refs)

        return pl.pallas_call(
            body,
            name="edge_masks",
            grid=(1,),
            out_shape=jax.ShapeDtypeStruct((slots // PARTS, 8, 16, BLOCK), BF),
            in_specs=[
                smem,
                pl.BlockSpec((slots // PARTS, 16, BLOCK), lambda i: (part, 0, 0)),
                vmem,
            ],
            out_specs=vmem,
            compiler_params=params,
        )(count, words, spread)

    moves = []
    for d in range(dst_count):
        for s in range(src_count):
            moves.append((d * src_count + s, s * dst_count + d))
    own_feats = lax.ppermute(features, ("dst", "src"), moves)
    near = [features if dy == 0 else shift(features, dy, 0) for dy in Y_STEPS]
    count = block_counts[0]
    masks = [masks_of(0, count), masks_of(1, count)]
    near, masks, count, own_feats = lax.optimization_barrier((near, masks, count, own_feats))
    column = jnp.concatenate(near, axis=0)
    arrived = {0: column, 1: shift(column, 0, 1), 7: shift(column, 0, 7)}
    own_terms, wst = pl.pallas_call(
        terms_kernel,
        name="own_terms",
        out_shape=[
            jax.ShapeDtypeStruct((2 * HEADS, own_rows), F32),
            jax.ShapeDtypeStruct((2 * HEADS, features.shape[1]), BF),
        ],
        in_specs=[vmem] * 4,
        out_specs=[vmem, vmem],
        compiler_params=params,
    )(own_feats, projection, jnp.stack([target_att, source_att]), head_fan)
    masks += [masks_of(2, count), masks_of(3, count)]
    arrived[1], arrived[7], own_terms, masks, count = lax.optimization_barrier(
        (arrived[1], arrived[7], own_terms, masks, count)
    )
    arrived[2], arrived[6] = shift(arrived[1], 0, 1), shift(arrived[7], 0, 7)
    row_terms = lax.all_to_all(
        jnp.broadcast_to(own_terms[None], (src_count,) + own_terms.shape), "src", 0, 0
    )
    arrived[2], arrived[6], row_terms, count = lax.optimization_barrier(
        (arrived[2], arrived[6], row_terms, count)
    )
    arrived[3], arrived[5] = shift(arrived[2], 0, 1), shift(arrived[6], 0, 7)
    factor_shape = (row_blocks, HEADS, 8, 16, BLOCK)
    factors = pl.pallas_call(
        factor_kernel,
        name="row_factors",
        out_shape=jax.ShapeDtypeStruct(factor_shape, BF),
        in_specs=[vmem] * 2,
        out_specs=vmem,
        compiler_params=params,
    )(row_terms, fan)
    arrived[3], arrived[5], factors = lax.optimization_barrier(
        (arrived[3], arrived[5], factors)
    )
    middle = column.shape[0] // 2
    last = [shift(arrived[3][:middle], 0, 1), shift(arrived[5][middle:], 0, 7)]
    at_dst, at_src = lax.axis_index("dst"), lax.axis_index("src")
    place = jnp.stack([at_dst // 8, at_dst % 8, at_src // 2, at_src % 2]).astype(jnp.int32)
    part_shape = jax.ShapeDtypeStruct((own_rows + AUX, WIDTH), BF)
    parts = pl.pallas_call(
        block_kernel,
        name="edge_blocks",
        out_shape=[part_shape] * src_count,
        in_specs=[smem] * 3 + [vmem] * (len(PIECES) + 3) + [anywhere] * (PARTS + 1) + [vmem] * 3,
        out_specs=[vmem] * src_count,
        scratch_shapes=[
            pltpu.VMEM((nodes, WIDTH), BF),
            pltpu.VMEM((HEADS, nodes), F32),
            pltpu.VMEM((nodes // BLOCK, HEADS, BLOCK), F32),
            pltpu.VMEM((nodes // BLOCK, HEADS, BLOCK), F32),
            pltpu.VMEM((slots, 8, 16, BLOCK), BF),
            pltpu.VMEM(factor_shape, BF),
        ]
        + [pltpu.VMEM((row_blocks, BLOCK, BLOCK), F32)] * 3
        + [pltpu.VMEM((src_count, HEADS, own_rows), F32)] * 2
        + [pltpu.VMEM((rows, HEADS), F32)] * 3
        + [pltpu.SemaphoreType.DMA((PARTS + 1,))],
        compiler_params=params,
    )(
        block_coords[0, 0], count, place, *[arrived[dz] for dz, _ in PIECES[:7]], *last,
        projection, wst, row_terms, *masks, factors, keep, ones, pick,
    )
    swap = [(i, i ^ 1) for i in range(src_count)]
    got = [lax.ppermute(x, "src", swap) for x in parts[:4]]
    sums = []
    for k, kept, other in zip(X_STEPS, parts[4:], got):
        x = pl.pallas_call(
            pair_kernel,
            name="pair_sums",
            out_shape=part_shape,
            in_specs=[vmem] * 3,
            out_specs=vmem,
            compiler_params=params,
        )(kept, other, head_fan)
        if k:
            x = lax.ppermute(
                x, "src", [(i, (i + 2 * k) % src_count) for i in range(src_count)]
            )
        sums.append(x)
    return pl.pallas_call(
        combine_kernel,
        name="combine_rows",
        out_shape=jax.ShapeDtypeStruct((own_rows, WIDTH), BF),
        in_specs=[vmem] * 9,
        out_specs=vmem,
        compiler_params=params,
    )(*sums, own_feats, projection, own_terms, out_bias[None], head_fan)


def solution(mesh):
    placed = (
        P(("src", "dst"), None),
        P(),
        P(),
        P(),
        P(),
        P("dst", "src", None, None),
        P("dst", "src", None, None, None),
        P("dst", "src"),
    )
    return jax.shard_map(
        on_device, mesh=mesh, in_specs=placed, out_specs=P(("dst", "src"), None), check_vma=False
    )
```

```python
import jax
import jax.numpy as jnp
import numpy as np
from jax import lax
from jax.experimental import pallas as pl
from jax.experimental.pallas import tpu as pltpu
from jax.sharding import PartitionSpec as P

HEADS = 8
HEAD_DIM = 32
BLOCK = 128
WIDTH = HEADS * HEAD_DIM
AUX = 48
STRIDE = 8
PARTS = 4
Y_STEPS = (0, 1, 3, 2)
PIECES = tuple((dz, Y_STEPS) for dz in (0, 1, 7, 2, 6, 3, 5)) + ((4, Y_STEPS[:2]), (4, Y_STEPS[2:]))
X_STEPS = (2, 1, 3, 0)
LOWEST = -3.0e38
BF = jnp.bfloat16
F32 = jnp.float32
NT = (((1,), (1,)), ((), ()))
TN = (((0,), (0,)), ((), ()))


def leaky(v):
    return jnp.maximum(v, 0.2 * v)


def constants():
    spread = np.zeros((16, BLOCK), np.float32)
    for b in range(BLOCK):
        spread[b // 8, b] = 0.5 ** (b % 8)
    keep = np.zeros((2, 16, BLOCK), np.float32)
    ones = np.zeros((2, 2, BLOCK, BLOCK), np.float32)
    for p in range(2):
        for lane in range(BLOCK):
            keep[p, :, lane] = float((lane % 64) // 32 == p)
        for t in range(2):
            ones[t, p, :, 4 * t + p] = 1.0
            ones[t, p, :, 4 * t + 2 + p] = 1.0
    pick = np.zeros((HEADS, BLOCK), np.float32)
    fan = np.zeros((HEADS, HEADS * BLOCK), np.float32)
    head_fan = np.zeros((2 * HEADS, WIDTH), np.float32)
    for h in range(HEADS):
        pick[h, h] = 1.0
        fan[h, h * BLOCK : (h + 1) * BLOCK] = 1.0
        head_fan[h, h * 32 : h * 32 + 32] = 1.0
        head_fan[HEADS + h, h * 32 : h * 32 + 32] = 1.0
    return [jnp.asarray(x, BF) for x in (spread, keep, ones, fan, pick, head_fan)]


def halves(x):
    high = x.astype(BF).astype(F32)
    return high, (x - high).astype(BF).astype(F32)


def terms_kernel(feats, proj, atts, head_fan, terms, wst):
    weights = proj[...].astype(F32)
    fold = head_fan[:HEADS, :].astype(F32)
    folded = [
        lax.dot_general(
            fold, weights * atts[k : k + 1, :], NT,
            precision=lax.Precision.HIGHEST, preferred_element_type=F32,
        )
        for k in range(2)
    ]
    terms[...] = lax.dot_general(
        jnp.concatenate(folded, axis=0), feats[...].astype(F32), NT,
        precision=lax.Precision.HIGHEST, preferred_element_type=F32,
    )
    high, low = halves(folded[1])
    wst[...] = jnp.concatenate([high, low], axis=0).astype(BF)


def mask_kernel(part, count, words, spread, masks):
    slots = masks.shape[0]
    live = jnp.clip(count[0] - part * slots, 0, slots)

    def edges(i, _):
        for k in range(STRIDE):
            slot = i * STRIDE + k
            w = words[slot] * jnp.where(slot < live, 1, 0)
            x = lax.dot_general(
                w.astype(F32).astype(BF), spread[...], TN, preferred_element_type=F32
            )
            bits = (x.astype(jnp.int32) & 1).astype(F32).astype(BF)
            masks[slot] = bits.reshape(8, 16, BLOCK)
        return 0

    lax.fori_loop(0, pl.cdiv(live, STRIDE), edges, 0)


def source_marks(terms):
    return jnp.max(jnp.max(terms[:, HEADS:, :], axis=0), axis=1, keepdims=True)


def factor_kernel(terms, fan, factors):
    mark = source_marks(terms)
    shards, _, own = terms.shape
    per = own // BLOCK
    for j in range(shards):
        factor = jnp.exp(jnp.minimum(-0.8 * (terms[j, :HEADS, :] + mark), 80.0)).astype(BF)
        for k in range(per):
            wide = lax.dot_general(
                factor[:, k * BLOCK : (k + 1) * BLOCK], fan[...], TN, preferred_element_type=F32
            ).astype(BF)
            for h in range(HEADS):
                factors[j * per + k, h] = wide[:, h * BLOCK : (h + 1) * BLOCK].reshape(8, 16, BLOCK)


def block_kernel(coords, count, place, *refs):
    pieces = refs[: len(PIECES)]
    refs = refs[len(PIECES) :]
    proj, wst, terms = refs[:3]
    masks_in = refs[3 : 3 + PARTS]
    (
        factors_in, keep, ones, pick,
        *outs, values, src, src_a, src_b, masks, factors, acc0, acc1, acc_d,
        hi, lo, col_t, col_s, col_m, sems,
    ) = refs[3 + PARTS :]
    accs = (acc0, acc1)
    piece_rows = pieces[0].shape[0] // len(Y_STEPS)
    shards, _, own = terms.shape
    per = own // BLOCK
    row_blocks = shards * per
    live = count[0]
    part = masks.shape[0] // PARTS
    copies = [
        pltpu.make_async_copy(masks_in[k], masks.at[k * part : (k + 1) * part], sems.at[k])
        for k in range(PARTS)
    ]
    copies.append(pltpu.make_async_copy(factors_in, factors, sems.at[PARTS]))
    for copy in copies:
        copy.start()

    zero = jnp.zeros((BLOCK, BLOCK), F32)
    for k, (dz, y_steps) in enumerate(PIECES):
        for m, dy in enumerate(y_steps):
            y = (place[0] + 4 - dy) % 4
            z = (place[1] + 8 - dz) % 8
            at = pl.ds(pl.multiple_of((y * 8 + z) * piece_rows, piece_rows), piece_rows)
            f = pieces[k][m * piece_rows : (m + 1) * piece_rows, :]
            values[at, :] = jnp.dot(f, proj[...], preferred_element_type=F32).astype(BF)
            both = lax.dot_general(wst[...], f, NT, preferred_element_type=F32)
            src[:, at] = both[:HEADS] + both[HEADS:]
    for r in range(row_blocks):
        for acc in (acc0, acc1, acc_d):
            acc[r] = zero

    top = jnp.max(src[...], axis=1, keepdims=True)
    mark = source_marks(terms)
    self_low = jnp.min(jnp.min(terms[:, HEADS:, :], axis=0), axis=1, keepdims=True)
    row_low = jnp.min(jnp.min(terms[:, :HEADS, :], axis=0), axis=1, keepdims=True) + mark
    narrow = (
        (jnp.max(top - mark) <= 40.0)
        & (jnp.max(mark - self_low) <= 60.0)
        & (jnp.min(row_low) >= -50.0)
    )
    for copy in copies:
        copy.wait()

    lane = lax.broadcasted_iota(jnp.int32, (BLOCK, BLOCK), 1)
    left = lane < 64
    second = (lane & 2) > 0

    def slot_of(slot):
        used = slot < live
        r = jnp.where(used, coords[0, slot], 0)
        q = jnp.where(used, coords[1, slot], 0)
        return r, q

    def nodes_of(q):
        return pl.ds(pl.multiple_of(q * BLOCK, BLOCK), BLOCK)

    def add_block(r, q, weight_of):
        dens = []
        for t in range(2):
            ws = [weight_of(h) for h in range(4 * t, 4 * t + 4)]
            lhs = jnp.concatenate(
                [jnp.concatenate(ws[:2], axis=1), jnp.concatenate(ws[2:], axis=1)], axis=0
            )
            vt = values[nodes_of(q), t * BLOCK : (t + 1) * BLOCK].reshape(8, 16, BLOCK)
            kept = jnp.concatenate(
                [
                    jnp.where(keep[p][None] > 0, vt, jnp.zeros_like(vt)).reshape(BLOCK, BLOCK)
                    for p in range(2)
                ],
                axis=0,
            )
            rhs = jnp.concatenate([kept, ones[t].reshape(2 * BLOCK, BLOCK)], axis=1)
            x = jnp.dot(lhs, rhs, preferred_element_type=F32)
            dens.append(jnp.where(second, x[BLOCK:, BLOCK:], x[:BLOCK, BLOCK:]))
            accs[t][r] += jnp.where(left, x[:BLOCK, :BLOCK], x[BLOCK:, :BLOCK])
        acc_d[r] += dens[0] + dens[1]

    @pl.when(narrow)
    def _():
        for b in range(src_a.shape[0]):
            gap = src[:, b * BLOCK : (b + 1) * BLOCK] - mark
            src_a[b] = jnp.exp(gap)
            src_b[b] = jnp.exp(0.2 * gap)
        for j in range(shards):
            high, low = halves(terms[j, :HEADS, :] + mark)
            hi[j] = high
            lo[j] = low

        def step(i, _):
            for k in range(STRIDE):
                slot = i * STRIDE + k
                r, q = slot_of(slot)

                def weight_of(h):
                    a = src_a[q, pl.ds(h, 16, stride=0), :].astype(BF)[None]
                    b = src_b[q, pl.ds(h, 16, stride=0), :].astype(BF)[None]
                    w = jnp.maximum(factors[r, h] * b, a) * masks[slot]
                    return w.reshape(BLOCK, BLOCK)

                add_block(r, q, weight_of)
            return 0

        lax.fori_loop(0, pl.cdiv(live, STRIDE), step, 0)

    @pl.when(jnp.logical_not(narrow))
    def _():
        col_s[...] = jnp.full(col_s.shape, LOWEST, F32)

        def edge_of(slot):
            return masks[slot].reshape(BLOCK, BLOCK).astype(F32) > 0

        def masked_max(slot, _):
            r, q = slot_of(slot)
            edge = edge_of(slot)
            s = src[:, nodes_of(q)]
            best = [
                jnp.max(jnp.where(edge, s[h : h + 1, :], LOWEST), axis=1, keepdims=True)
                for h in range(HEADS)
            ]
            at = nodes_of(r)
            col_s[at, :] = jnp.maximum(col_s[at, :], jnp.concatenate(best, axis=1))
            return 0

        lax.fori_loop(0, live, masked_max, 0)
        for r in range(row_blocks):
            at = slice(r * BLOCK, (r + 1) * BLOCK)
            j = r // per
            inner = slice((r % per) * BLOCK, (r % per + 1) * BLOCK)
            t = terms[j, :HEADS, inner]
            exact = jnp.maximum(leaky(t + terms[j, HEADS:, inner]), leaky(t + col_s[at, :].T))
            high, low = halves(exact)
            hi[j, :, inner] = high
            lo[j, :, inner] = low
            col_m[at, :] = (high + low).T
            col_t[at, :] = t.T

        def step(slot, _):
            r, q = slot_of(slot)
            edge = edge_of(slot)
            s = src[:, nodes_of(q)]
            t = col_t[nodes_of(r), :]
            m = col_m[nodes_of(r), :]

            def weight_of(h):
                score = leaky(t[:, h : h + 1] + s[h : h + 1, :]) - m[:, h : h + 1]
                return jnp.where(edge, jnp.exp(score), 0.0).astype(BF)

            add_block(r, q, weight_of)
            return 0

        lax.fori_loop(0, live, step, 0)

    for i, out in enumerate(outs):
        j = (place[2] + X_STEPS[i % 4]) % 4 * 2 + (1 - place[3] if i < 4 else place[3])
        dens = []
        for k in range(per):
            r = j * per + k
            at = slice(k * BLOCK, (k + 1) * BLOCK)
            out[at, :BLOCK] = acc0[r].astype(BF)
            out[at, BLOCK:] = acc1[r].astype(BF)
            dens.append(
                lax.dot_general(pick[...], acc_d[r].astype(BF), NT, preferred_element_type=F32)
            )
        out[own : own + 16, :] = flat(jnp.concatenate(dens, axis=1))
        out[own + 16 : own + 32, :] = flat(hi[j])
        out[own + 32 : own + 48, :] = flat(lo[j])


def tall(x):
    x = x.astype(F32)
    return jnp.concatenate([x[:HEADS], x[HEADS:]], axis=1)


def flat(x):
    half = x.shape[1] // 2
    return jnp.concatenate([x[:, :half], x[:, half:]], axis=0).astype(BF)


def fanned(x, head_fan):
    high, low = halves(x)
    both = jnp.concatenate([high, low], axis=0).astype(BF)
    return lax.dot_general(both, head_fan[...], TN, preferred_element_type=F32)


def pair_kernel(kept, got, head_fan, out):
    own = out.shape[0] - AUX
    read = (kept, got)
    den = [tall(x[own : own + 16, :]) for x in read]
    high = [tall(x[own + 16 : own + 32, :]) for x in read]
    low = [tall(x[own + 32 : own + 48, :]) for x in read]
    shift = [h + l for h, l in zip(high, low)]
    m = jnp.maximum(shift[0], shift[1])
    scale = [jnp.exp(x - m) for x in shift]
    total = sum(fanned(k, head_fan) * x[:own, :].astype(F32) for k, x in zip(scale, read))
    out[:own, :] = total.astype(BF)
    first = shift[0] >= shift[1]
    out[own : own + 16, :] = flat(scale[0] * den[0] + scale[1] * den[1])
    out[own + 16 : own + 32, :] = flat(jnp.where(first, high[0], high[1]))
    out[own + 32 : own + 48, :] = flat(jnp.where(first, low[0], low[1]))


def combine_kernel(*refs):
    parts = refs[:4]
    feats, proj, terms, bias, head_fan, out = refs[4:]
    own = feats.shape[0]
    dens, shifts = [], []
    for part in parts:
        dens.append(tall(part[own : own + 16, :]))
        shifts.append(tall(part[own + 16 : own + 32, :]) + tall(part[own + 32 : own + 48, :]))
    score = leaky(terms[:HEADS, :] + terms[HEADS:, :])
    m = score
    for s in shifts:
        m = jnp.maximum(m, s)
    own_weight = jnp.exp(score - m)
    total = own_weight
    scales = []
    for d, s in zip(dens, shifts):
        scale = jnp.exp(s - m)
        scales.append(scale)
        total = total + scale * d
    inverse = 1.0 / total
    values = jnp.dot(feats[...], proj[...], preferred_element_type=F32).astype(BF).astype(F32)
    mixed = fanned(own_weight * inverse, head_fan) * values + bias[...]
    for part, scale in zip(parts, scales):
        mixed = mixed + fanned(scale * inverse, head_fan) * part[:own, :].astype(F32)
    out[...] = jnp.where(mixed > 0, mixed, jnp.exp(jnp.minimum(mixed, 0.0)) - 1.0).astype(BF)


def on_device(
    features, projection, source_att, target_att, out_bias, block_coords, block_words, block_counts
):
    dst_count = lax.axis_size("dst")
    src_count = lax.axis_size("src")
    own_rows = features.shape[0]
    rows = own_rows * src_count
    nodes = own_rows * dst_count
    slots = block_coords.shape[3]
    row_blocks = rows // BLOCK
    spread, keep, ones, fan, pick, head_fan = constants()
    smem = pl.BlockSpec(memory_space=pltpu.SMEM)
    vmem = pl.BlockSpec(memory_space=pltpu.VMEM)
    anywhere = pl.BlockSpec(memory_space=pl.ANY)
    params = pltpu.CompilerParams(vmem_limit_bytes=60 * 2**20)
    words = block_words[0, 0]

    def shift(x, dy, dz):
        return lax.ppermute(
            x,
            "dst",
            [(y * 8 + z, (y + dy) % 4 * 8 + (z + dz) % 8) for y in range(4) for z in range(8)],
        )

    def masks_of(part, count):
        def body(*refs):
            mask_kernel(part, *refs)

        return pl.pallas_call(
            body,
            name="edge_masks",
            grid=(1,),
            out_shape=jax.ShapeDtypeStruct((slots // PARTS, 8, 16, BLOCK), BF),
            in_specs=[
                smem,
                pl.BlockSpec((slots // PARTS, 16, BLOCK), lambda i: (part, 0, 0)),
                vmem,
            ],
            out_specs=vmem,
            compiler_params=params,
        )(count, words, spread)

    moves = []
    for d in range(dst_count):
        for s in range(src_count):
            moves.append((d * src_count + s, s * dst_count + d))
    own_feats = lax.ppermute(features, ("dst", "src"), moves)
    near = [features if dy == 0 else shift(features, dy, 0) for dy in Y_STEPS]
    count = block_counts[0]
    masks = [masks_of(0, count)]
    near, masks[0], count = lax.optimization_barrier((near, masks[0], count))
    column = jnp.concatenate(near, axis=0)
    arrived = {0: column, 1: shift(column, 0, 1), 7: shift(column, 0, 7)}
    own_terms, wst = pl.pallas_call(
        terms_kernel,
        name="own_terms",
        out_shape=[
            jax.ShapeDtypeStruct((2 * HEADS, own_rows), F32),
            jax.ShapeDtypeStruct((2 * HEADS, features.shape[1]), BF),
        ],
        in_specs=[vmem] * 4,
        out_specs=[vmem, vmem],
        compiler_params=params,
    )(own_feats, projection, jnp.stack([target_att, source_att]), head_fan)
    masks.append(masks_of(1, count))
    arrived[1], arrived[7], own_terms, masks, count = lax.optimization_barrier(
        (arrived[1], arrived[7], own_terms, masks, count)
    )
    arrived[2], arrived[6] = shift(arrived[1], 0, 1), shift(arrived[7], 0, 7)
    row_terms = lax.all_to_all(
        jnp.broadcast_to(own_terms[None], (src_count,) + own_terms.shape), "src", 0, 0
    )
    arrived[2], arrived[6], row_terms, count = lax.optimization_barrier(
        (arrived[2], arrived[6], row_terms, count)
    )
    arrived[3], arrived[5] = shift(arrived[2], 0, 1), shift(arrived[6], 0, 7)
    factor_shape = (row_blocks, HEADS, 8, 16, BLOCK)
    factors = pl.pallas_call(
        factor_kernel,
        name="row_factors",
        out_shape=jax.ShapeDtypeStruct(factor_shape, BF),
        in_specs=[vmem] * 2,
        out_specs=vmem,
        compiler_params=params,
    )(row_terms, fan)
    masks.append(masks_of(2, count))
    arrived[3], arrived[5], factors, masks, count = lax.optimization_barrier(
        (arrived[3], arrived[5], factors, masks, count)
    )
    middle = column.shape[0] // 2
    last = [shift(arrived[3][:middle], 0, 1), shift(arrived[5][middle:], 0, 7)]
    masks.append(masks_of(3, count))
    at_dst, at_src = lax.axis_index("dst"), lax.axis_index("src")
    place = jnp.stack([at_dst // 8, at_dst % 8, at_src // 2, at_src % 2]).astype(jnp.int32)
    part_shape = jax.ShapeDtypeStruct((own_rows + AUX, WIDTH), BF)
    parts = pl.pallas_call(
        block_kernel,
        name="edge_blocks",
        out_shape=[part_shape] * src_count,
        in_specs=[smem] * 3 + [vmem] * (len(PIECES) + 3) + [anywhere] * (PARTS + 1) + [vmem] * 3,
        out_specs=[vmem] * src_count,
        scratch_shapes=[
            pltpu.VMEM((nodes, WIDTH), BF),
            pltpu.VMEM((HEADS, nodes), F32),
            pltpu.VMEM((nodes // BLOCK, HEADS, BLOCK), F32),
            pltpu.VMEM((nodes // BLOCK, HEADS, BLOCK), F32),
            pltpu.VMEM((slots, 8, 16, BLOCK), BF),
            pltpu.VMEM(factor_shape, BF),
        ]
        + [pltpu.VMEM((row_blocks, BLOCK, BLOCK), F32)] * 3
        + [pltpu.VMEM((src_count, HEADS, own_rows), F32)] * 2
        + [pltpu.VMEM((rows, HEADS), F32)] * 3
        + [pltpu.SemaphoreType.DMA((PARTS + 1,))],
        compiler_params=params,
    )(
        block_coords[0, 0], count, place, *[arrived[dz] for dz, _ in PIECES[:7]], *last,
        projection, wst, row_terms, *masks, factors, keep, ones, pick,
    )
    swap = [(i, i ^ 1) for i in range(src_count)]
    got = [lax.ppermute(x, "src", swap) for x in parts[:4]]
    sums = []
    for k, kept, other in zip(X_STEPS, parts[4:], got):
        x = pl.pallas_call(
            pair_kernel,
            name="pair_sums",
            out_shape=part_shape,
            in_specs=[vmem] * 3,
            out_specs=vmem,
            compiler_params=params,
        )(kept, other, head_fan)
        if k:
            x = lax.ppermute(
                x, "src", [(i, (i + 2 * k) % src_count) for i in range(src_count)]
            )
        sums.append(x)
    return pl.pallas_call(
        combine_kernel,
        name="combine_rows",
        out_shape=jax.ShapeDtypeStruct((own_rows, WIDTH), BF),
        in_specs=[vmem] * 9,
        out_specs=vmem,
        compiler_params=params,
    )(*sums, own_feats, projection, own_terms, out_bias[None], head_fan)


def solution(mesh):
    placed = (
        P(("src", "dst"), None),
        P(),
        P(),
        P(),
        P(),
        P("dst", "src", None, None),
        P("dst", "src", None, None, None),
        P("dst", "src"),
    )
    return jax.shard_map(
        on_device, mesh=mesh, in_specs=placed, out_specs=P(("dst", "src"), None), check_vma=False
    )
```
